32 devices in a mesh: dp: 4 (over z), gx: 2 (over core), gy: 4 (over y, x).
Axes of the slice: x: 2, y: 2, z: 4, core: 2. Of those that a mesh axis runs over, the one named last changes fastest.
Arguments:
- layer_input: bfloat16 [16384, 1280], P(('dp', 'gx', 'gy')), may hold values from -6 to 6
- first_gain: float32 [1280], P('gy'), may hold values from 0.5 to 1.5
- query_scale: float32 [80], replicated, may hold values from -1 to 1
- query_weight: bfloat16 [1280, 1280], P('gy', 'gx'), may hold values from -0.15625 to 0.15625
- key_weight: bfloat16 [1280, 1280], P('gy', 'gx'), may hold values from -0.15625 to 0.15625
- value_weight: bfloat16 [1280, 1280], P('gy', 'gx'), may hold values from -0.15625 to 0.15625
- output_weight: bfloat16 [1280, 1280], P('gx', 'gy'), may hold values from -2 to 2
- second_gain: float32 [1280], P('gy'), may hold values from 0.5 to 1.5
- inner_weight: bfloat16 [1280, 1280], P('gy', 'gx'), may hold values from -0.15625 to 0.15625
- inner_bias: float32 [1280], P('gx'), may hold values from -3 to 3
- outer_weight: bfloat16 [1280, 1280], P('gx', 'gy'), may hold values from -0.15625 to 0.15625
- outer_bias: float32 [1280], P('gy'), may hold values from -3 to 3
- prefix_len: int32 [4], replicated, may hold values from 409 to 2048
- output_cotangent: bfloat16 [16384, 1280], P(('dp', 'gx', 'gy')), may hold values from -6 to 6
Outputs:
- layer_output: bfloat16 [16384, 1280], P(('dp', 'gx', 'gy'))
- input_gradient: bfloat16 [16384, 1280], P(('dp', 'gx', 'gy'))
- first_gain_gradient: float32 [1280], P('gy')
- query_scale_gradient: float32 [80], replicated
- query_weight_gradient: float32 [1280, 1280], P('gy', 'gx')
- key_weight_gradient: float32 [1280, 1280], P('gy', 'gx')
- value_weight_gradient: float32 [1280, 1280], P('gy', 'gx')
- output_weight_gradient: float32 [1280, 1280], P('gx', 'gy')
- second_gain_gradient: float32 [1280], P('gy')
- inner_weight_gradient: float32 [1280, 1280], P('gy', 'gx')
- inner_bias_gradient: float32 [1280], P('gx')
- outer_weight_gradient: float32 [1280, 1280], P('gx', 'gy')
- outer_bias_gradient: float32 [1280], P('gy')
The draws below stay inside these ranges and needn't reach their ends.
Inputs may be any that keep to these rules, and one draw needn't show every extreme that they name: Each sequence's first prefix_len positions are seen by all its queries.
All inputs are finite; a program needn't handle non-finite values.
Results may differ from the reference program's by a relative error of at most 0.018.
Values may be sent and summed in bfloat16 or wider, within the bound.
A program may use at most 448 MiB of HBM per device.

```python
import math
import jax
import jax.numpy as jnp
from jax import lax

D = 1280
H = 16
DH = 80
F = 1280
HD = 1280
LEN = 4096
SEQS = 4
TOKENS = 16384


def place_ends(array, own_key, smallest, high):
    shape = array.shape
    spot = [jax.random.randint(jax.random.fold_in(own_key, axis), (), 0, shape[axis]) for axis in range(len(shape))]
    array = array.at[tuple(spot)].set(smallest)
    longest = shape.index(max(shape))
    spot[longest] = (spot[longest] + 1) % shape[longest]
    return array.at[tuple(spot)].set(high)


def levels(rng, shape, cuts, least, top_value):
    def one(position, shards_of):
        steps = jax.random.uniform(jax.random.fold_in(jax.random.fold_in(rng, 6), position), (shards_of,), jnp.float32, least / len(cuts), top_value / len(cuts))
        return jnp.repeat(jnp.exp(steps), shape[position] // shards_of).reshape((-1,) + (1,) * (len(shape) - position - 1))

    level = one(*cuts[0])
    for cut in cuts[1:]:
        level = level * one(*cut)
    return level


def bell_draw(key, shape, scale, reach, cuts=(), kind=jnp.bfloat16):
    values = jax.random.normal(key, shape, jnp.float32) * scale
    if len(cuts) > 0:
        values = levels(key, shape, cuts, -0.22, 0.18) * values
    return jnp.clip(values, min=-reach, max=reach).astype(kind)


def setup_inputs(seed: int = 0) -> dict:
    seeds = jax.random.split(jax.random.key(seed), 15)
    return {
        "layer_input": bell_draw(seeds[0], (TOKENS, D), 1.0, 6.0, ((0, 32),)),
        "first_gain": jnp.clip(1.0 + 0.1 * jax.random.normal(seeds[1], (D,), jnp.float32), 0.5, 1.5),
        "query_scale": jnp.clip(jax.random.uniform(seeds[2], (DH,), jnp.float32, -1.0, 1.0), -1.0, 1.0),
        "query_weight": bell_draw(seeds[3], (D, HD), D ** -0.5, 0.15625, ((0, 4), (1, 2))),
        "key_weight": bell_draw(seeds[4], (D, HD), D ** -0.5, 0.15625, ((0, 4), (1, 2))),
        "value_weight": bell_draw(seeds[5], (D, HD), D ** -0.5, 0.15625, ((0, 4), (1, 2))),
        "output_weight": bell_draw(seeds[6], (HD, D), (max(1, HD * 32 // LEN)) ** -0.5, 2.0, ((0, 2), (1, 4))),
        "second_gain": jnp.clip(1.0 + 0.1 * jax.random.normal(seeds[7], (D,), jnp.float32), 0.5, 1.5),
        "inner_weight": bell_draw(seeds[8], (D, F), D ** -0.5, 0.15625, ((0, 4), (1, 2))),
        "inner_bias": bell_draw(seeds[9], (F,), 0.5, 3.0, ((0, 2),), jnp.float32),
        "outer_weight": bell_draw(seeds[10], (F, D), F ** -0.5, 0.15625, ((0, 2), (1, 4))),
        "outer_bias": bell_draw(seeds[11], (D,), 0.5, 3.0, ((0, 4),), jnp.float32),
        "prefix_len": place_ends(jax.random.randint(seeds[12], (SEQS,), LEN // 10, LEN // 2 + 1), jax.random.fold_in(seeds[12], 1), LEN // 10, (LEN // 2 + 1) - 1).astype(jnp.int32),
        "output_cotangent": bell_draw(seeds[13], (TOKENS, D), 1.0, 6.0, ((0, 32),)),
    }


@jax.custom_vjp
def low(v):
    return lax.optimization_barrier(v.astype(jnp.bfloat16)).astype(jnp.float32)

@jax.custom_vjp
def low_back(v):
    return v

def low_keep(v):
    return (low(v), None)

def low_pass(kept, grad):
    return (grad,)

def back_keep(v):
    return (v, None)

def back_low(kept, grad):
    return (low(grad),)
low.defvjp(low_keep, low_pass)
low_back.defvjp(back_keep, back_low)
softplus_unit = 1.442695041

def product(left, right):
    return jnp.dot(left, right, precision=lax.Precision.HIGHEST)

def normalize(values, gain):
    inverse = lax.rsqrt(lax.optimization_barrier(jnp.mean(values * values, axis=-1, keepdims=True)) + 1e-06)
    return values * inverse * gain

def attend_sequence(queries, keys, values, prefix):
    block = min(512, LEN)

    def one_block(start):
        rows = lax.dynamic_slice_in_dim(queries, start, block, 0)
        scores = low_back(jnp.einsum('qhd,khd->hqk', rows, keys, precision=lax.Precision.HIGHEST))
        place = start + jnp.arange(block, dtype=jnp.int32)[:, None]
        column = jnp.arange(LEN, dtype=jnp.int32)[None, :]
        allowed = (column <= place) | (column < prefix)
        scores = jnp.where(allowed[None], scores, -1e+30)
        weights = jax.nn.softmax(scores, axis=-1)
        return jnp.einsum('hqk,khd->qhd', low(weights), values, precision=lax.Precision.HIGHEST)
    starts = jnp.arange(LEN // block, dtype=jnp.int32) * block
    return lax.map(jax.checkpoint(one_block), starts).reshape(LEN, H, DH)

def layer(inputs, first_gain, query_scale, query_weight, key_weight, value_weight, output_weight, second_gain, inner_weight, inner_bias, outer_weight, outer_bias, prefix_len):
    normed = low(normalize(inputs, first_gain))
    queries = low_back(product(normed, query_weight))
    keys = low_back(low(product(normed, key_weight)))
    values = low_back(low(product(normed, value_weight)))
    factor = jax.nn.softplus(query_scale) * (softplus_unit / math.sqrt(DH))
    scaled = low(queries.reshape(SEQS, LEN, H, DH) * factor)

    def per_sequence(group):
        return attend_sequence(group[0], group[1], group[2], group[3])
    mixed = lax.map(per_sequence, (scaled, keys.reshape(SEQS, LEN, H, DH), values.reshape(SEQS, LEN, H, DH), prefix_len))
    attended = low_back(low(mixed.reshape(TOKENS, HD)))
    middle = inputs + low_back(product(attended, output_weight))
    normed_two = low(normalize(middle, second_gain))
    before = low_back(product(normed_two, inner_weight)) + inner_bias
    hidden = low(jax.nn.silu(before))
    return middle + low_back(product(hidden, outer_weight)) + outer_bias

def reference(layer_input, first_gain, query_scale, query_weight, key_weight, value_weight, output_weight, second_gain, inner_weight, inner_bias, outer_weight, outer_bias, prefix_len, output_cotangent):
    floats = (layer_input.astype(jnp.float32), first_gain.astype(jnp.float32), query_scale.astype(jnp.float32), query_weight.astype(jnp.float32), key_weight.astype(jnp.float32), value_weight.astype(jnp.float32), output_weight.astype(jnp.float32), second_gain.astype(jnp.float32), inner_weight.astype(jnp.float32), inner_bias.astype(jnp.float32), outer_weight.astype(jnp.float32), outer_bias.astype(jnp.float32))

    def closed(*arrays):
        return layer(*arrays, prefix_len)
    result, pull = jax.vjp(closed, *floats)
    grads = pull(output_cotangent.astype(jnp.float32))
    return (result.astype(jnp.bfloat16), grads[0].astype(jnp.bfloat16), grads[1], grads[2], grads[3], grads[4], grads[5], grads[6], grads[7], grads[8], grads[9], grads[10], grads[11])
```

```python
import functools
import math

import jax
import jax.numpy as jnp
from jax import lax
from jax.experimental import pallas as pl
from jax.experimental.pallas import tpu as pltpu
from jax.sharding import PartitionSpec as P

DH = 80
softplus_unit = 1.442695041
NN = (((1,), (0,)), ((), ()))
NT = (((1,), (1,)), ((), ()))
TN = (((0,), (0,)), ((), ()))


def dot(left, right, how):
    return lax.dot_general(left, right, how, preferred_element_type=jnp.float32)


def visible(scores, i, j, bq, bk, prefix):
    key = j * bk + lax.broadcasted_iota(jnp.int32, scores.shape, 0)
    query = i * bq + lax.broadcasted_iota(jnp.int32, scores.shape, 1)
    return jnp.where((key <= query) | (key < prefix), scores, -1e30)


def block_range(i, bq, bk, prefix):
    whole = jnp.maximum((i * bq + 1) // bk, prefix // bk)
    seen = jnp.maximum(((i + 1) * bq + bk - 1) // bk, (prefix + bk - 1) // bk)
    return whole, seen


def forward_kernel(bq, bk, heads, prefix_ref, q_t, k, v_t, o_t, lse):
    i = pl.program_id(0)
    prefix = prefix_ref[0]
    whole, seen = block_range(i, bq, bk, prefix)

    def step(masked, j, carry):
        out = []
        rows = pl.ds(pl.multiple_of(j * bk, bk), bk)
        scores = [dot(k[h, rows, :], q_t[h], NN) for h in range(heads)]
        for h in range(heads):
            largest, total, mixed = carry[h]
            s = visible(scores[h], i, j, bq, bk, prefix) if masked else scores[h]
            now = jnp.maximum(largest, jnp.max(s, axis=0, keepdims=True))
            raised = jnp.exp(s - now)
            shrink = jnp.exp(largest - now)
            total = total * shrink + jnp.sum(raised, axis=0, keepdims=True)
            mixed = mixed * shrink + dot(v_t[h, :, rows], raised.astype(jnp.bfloat16), NN)
            out.append((now, total, mixed))
        return tuple(out)

    start = tuple(
        (
            jnp.full((1, bq), -1e30, jnp.float32),
            jnp.zeros((1, bq), jnp.float32),
            jnp.zeros((DH, bq), jnp.float32),
        )
        for _ in range(heads)
    )
    done = lax.fori_loop(0, whole, functools.partial(step, False), start)
    done = lax.fori_loop(whole, seen, functools.partial(step, True), done)
    for h in range(heads):
        largest, total, mixed = done[h]
        o_t[h] = mixed / total
        lse[h] = largest + jnp.log(total)


def attention_forward(q_t, k, v_t, prefix):
    heads, _, length = q_t.shape
    bq = bk = min(512, length)
    columns = lambda n: pl.BlockSpec((heads, n, bq), lambda i, p: (0, 0, i))
    whole = lambda a: pl.BlockSpec(a.shape, lambda i, p: (0, 0, 0))
    return pl.pallas_call(
        functools.partial(forward_kernel, bq, bk, heads),
        grid_spec=pltpu.PrefetchScalarGridSpec(
            num_scalar_prefetch=1,
            grid=(length // bq,),
            in_specs=[columns(DH), whole(k), whole(v_t)],
            out_specs=[columns(DH), columns(1)],
        ),
        out_shape=[
            jax.ShapeDtypeStruct((heads, DH, length), jnp.float32),
            jax.ShapeDtypeStruct((heads, 1, length), jnp.float32),
        ],
        cost_estimate=pl.CostEstimate(
            flops=heads * length * length * 256 * 2,
            transcendentals=heads * length * length // 2,
            bytes_accessed=heads * length * DH * 12,
        ),
        name="attention_forward",
    )(prefix, q_t, k, v_t)


def backward_kernel(
    bq, bk, heads, count, prefix_ref, q_t, k, k_t, v, g_t, o_t, lse, dq_t, dk, dv, dk_sum, dv_sum
):
    i = pl.program_id(0)
    prefix = prefix_ref[0]
    whole, seen = block_range(i, bq, bk, prefix)

    @pl.when(i == 0)
    def _():
        dk_sum[...] = jnp.zeros_like(dk_sum)
        dv_sum[...] = jnp.zeros_like(dv_sum)

    centre = [
        jnp.sum(g_t[h].astype(jnp.float32) * o_t[h], axis=0, keepdims=True) for h in range(heads)
    ]

    def step(masked, j, carry):
        rows = pl.ds(pl.multiple_of(j * bk, bk), bk)
        out = []
        scores = [dot(k[h, rows, :], q_t[h], NN) for h in range(heads)]
        along = [dot(v[h, rows, :], g_t[h], NN) for h in range(heads)]
        for h in range(heads):
            s = visible(scores[h], i, j, bq, bk, prefix) if masked else scores[h]
            weights = jnp.exp(s - lse[h])
            low = (weights * (along[h] - centre[h])).astype(jnp.bfloat16)
            dv_sum[h, rows, :] += dot(weights.astype(jnp.bfloat16), g_t[h], NT)
            dk_sum[h, rows, :] += dot(low, q_t[h], NT)
            out.append(carry[h] + dot(k_t[h, :, rows], low, NN))
        return tuple(out)

    done = tuple(jnp.zeros((DH, bq), jnp.float32) for _ in range(heads))
    done = lax.fori_loop(0, whole, functools.partial(step, False), done)
    done = lax.fori_loop(whole, seen, functools.partial(step, True), done)
    for h in range(heads):
        dq_t[h] = done[h]

    @pl.when(i == count - 1)
    def _():
        dk[...] = dk_sum[...].astype(jnp.bfloat16)
        dv[...] = dv_sum[...].astype(jnp.bfloat16)


def attention_backward(q_t, k, k_t, v, g_t, o_t, lse, prefix):
    heads, _, length = q_t.shape
    bq = bk = min(512, length)
    columns = lambda n: pl.BlockSpec((heads, n, bq), lambda i, p: (0, 0, i))
    whole = lambda a: pl.BlockSpec(a.shape, lambda i, p: (0, 0, 0))
    return pl.pallas_call(
        functools.partial(backward_kernel, bq, bk, heads, length // bq),
        grid_spec=pltpu.PrefetchScalarGridSpec(
            num_scalar_prefetch=1,
            grid=(length // bq,),
            in_specs=[
                columns(DH), whole(k), whole(k_t), whole(v), columns(DH), columns(DH), columns(1)
            ],
            out_specs=[columns(DH), whole(k), whole(k)],
            scratch_shapes=[pltpu.VMEM(k.shape, jnp.float32)] * 2,
        ),
        out_shape=[
            jax.ShapeDtypeStruct(q_t.shape, jnp.float32),
            jax.ShapeDtypeStruct(k.shape, jnp.bfloat16),
            jax.ShapeDtypeStruct(k.shape, jnp.bfloat16),
        ],
        cost_estimate=pl.CostEstimate(
            flops=heads * length * length * 256 * 5,
            transcendentals=heads * length * length // 2,
            bytes_accessed=heads * length * DH * 24,
        ),
        name="attention_backward",
    )(prefix, q_t, k, k_t, v, g_t, o_t, lse)


def normalize(values, gain):
    inverse = lax.rsqrt(jnp.mean(values * values, axis=-1, keepdims=True) + 1e-06)
    unit = values * inverse
    return unit, inverse, (unit * gain).astype(jnp.bfloat16)


def normalize_back(upstream, unit, inverse, gain):
    scaled = upstream * gain
    mean = jnp.mean(scaled * unit, axis=-1, keepdims=True)
    return inverse * (scaled - unit * mean), jnp.sum(upstream * unit, axis=0)


def per_device(
    layer_input,
    first_gain,
    query_scale,
    query_weight,
    key_weight,
    value_weight,
    output_weight,
    second_gain,
    inner_weight,
    inner_bias,
    outer_weight,
    outer_bias,
    prefix_len,
    output_cotangent,
):
    gx, gy = lax.axis_size("gx"), lax.axis_size("gy")
    both = ("gx", "gy")
    rows, width = layer_input.shape
    group = rows * gx * gy
    all_heads = query_weight.shape[1] * gx // DH
    split = all_heads % (gx * gy) == 0
    heads = all_heads // (gx * gy if split else gy)
    assert prefix_len.shape[0] == lax.axis_size("dp")
    assert heads * (gx * gy if split else gy) == all_heads
    x_index, y_index = lax.axis_index("gx"), lax.axis_index("gy")
    prefix = lax.dynamic_slice_in_dim(prefix_len, lax.axis_index("dp"), 1, 0)

    def to_heads(columns):
        if split:
            return lax.all_to_all(columns, both, split_axis=0, concat_axis=1, tiled=True)
        half = lax.all_to_all(columns, "gy", split_axis=0, concat_axis=1, tiled=True)
        return lax.all_gather(half, "gx", axis=1, tiled=True)

    def to_tokens(columns):
        if split:
            return lax.all_to_all(columns, both, split_axis=1, concat_axis=0, tiled=True)
        half = lax.dynamic_slice_in_dim(columns, x_index * (group // gx), group // gx, 1)
        return lax.all_to_all(half, "gy", split_axis=1, concat_axis=0, tiled=True)

    def weight_to_heads(stack):
        if not split:
            stack = lax.all_gather(stack, "gx", axis=2, tiled=True)
        return lax.all_to_all(stack, "gy", split_axis=2, concat_axis=1, tiled=True)

    def weight_from_heads(stack):
        stack = lax.all_to_all(stack, "gy", split_axis=1, concat_axis=2, tiled=True)
        if not split:
            own = stack.shape[2] // gx
            stack = lax.dynamic_slice_in_dim(stack, x_index * own, own, 2)
        return stack

    everyone = lax.all_gather(lax.all_gather(layer_input, "gy", axis=0, tiled=True), "gx", axis=0, tiled=True)
    own_weights = weight_to_heads(jnp.stack([query_weight, key_weight, value_weight]))
    gains = lax.all_gather(jnp.stack([first_gain, second_gain, outer_bias]), "gy", axis=1, tiled=True)
    inner_bias_all = lax.all_gather(inner_bias, "gx", axis=0, tiled=True)
    first_gain_all, second_gain_all, outer_bias_all = gains[0], gains[1], gains[2]

    late = jnp.stack([output_weight.T, inner_weight, outer_weight.T])
    late = lax.all_gather(lax.all_gather(late, "gy", axis=1, tiled=True), "gx", axis=2, tiled=True)
    output_all, inner_all, outer_all = late[0], late[1], late[2]

    _, _, normed_one = normalize(everyone.astype(jnp.float32), first_gain_all)
    factor = jax.nn.softplus(query_scale) * (softplus_unit / math.sqrt(DH))
    own = heads * DH
    wq, wk, wv = own_weights[0], own_weights[1], own_weights[2]
    turned = dot(jnp.concatenate([wq, wk, wv], axis=1), normed_one, (((0,), (1,)), ((), ())))
    queries_t = turned[:own].reshape(heads, DH, group)
    k_t = turned[own : 2 * own].reshape(heads, DH, group).astype(jnp.bfloat16)
    v_t = turned[2 * own :].reshape(heads, DH, group).astype(jnp.bfloat16)
    q_t = (queries_t * factor[None, :, None]).astype(jnp.bfloat16)
    k = jnp.swapaxes(k_t, 1, 2)
    v = jnp.swapaxes(v_t, 1, 2)
    o_t, lse = attention_forward(q_t, k, v_t, prefix)
    attended = to_tokens(o_t.reshape(own, group).astype(jnp.bfloat16))

    inputs = layer_input.astype(jnp.float32)
    middle = inputs + dot(attended, output_all, (((0,), (1,)), ((), ())))
    unit_two, inverse_two, normed_two = normalize(middle, second_gain_all)
    before = dot(normed_two, inner_all, NN) + inner_bias_all
    sigmoid = jax.nn.sigmoid(before)
    hidden = (before * sigmoid).astype(jnp.bfloat16)
    layer_output = (middle + dot(hidden, outer_all, NT) + outer_bias_all).astype(jnp.bfloat16)

    upstream = output_cotangent.astype(jnp.float32)
    hidden_gradient = dot(output_cotangent, outer_all, NN)
    before_gradient = hidden_gradient * sigmoid * (1.0 + before * (1.0 - sigmoid))
    before_low = before_gradient.astype(jnp.bfloat16)
    middle_part, second_gain_part = normalize_back(
        dot(before_low, inner_all, NT), unit_two, inverse_two, second_gain_all
    )
    middle_gradient = upstream + middle_part
    branch_low = middle_gradient.astype(jnp.bfloat16)
    g_t = to_heads(dot(output_all, branch_low, (((0,), (1,)), ((), ()))).astype(jnp.bfloat16))

    late_gradient = jnp.stack(
        [
            dot(branch_low, attended, (((0,), (1,)), ((), ()))).astype(jnp.bfloat16),
            dot(normed_two, before_low, TN).astype(jnp.bfloat16),
            dot(output_cotangent, hidden, TN).astype(jnp.bfloat16),
        ]
    )
    late_gradient = lax.psum_scatter(late_gradient, "gx", scatter_dimension=2, tiled=True)
    late_gradient = lax.psum_scatter(late_gradient, "gy", scatter_dimension=1, tiled=True)
    late_gradient = lax.psum(late_gradient, "dp").astype(jnp.float32)

    dq_t, dk, dv = attention_backward(
        q_t, k, k_t, v, g_t.reshape(heads, DH, group), o_t, lse, prefix
    )
    scale_part = jnp.sum(dq_t * queries_t, axis=(0, 2))
    if not split:
        scale_part = scale_part / gx
    joined = jnp.concatenate(
        [
            (dq_t * factor[None, :, None]).astype(jnp.bfloat16).reshape(own, group),
            jnp.swapaxes(dk, 1, 2).reshape(own, group),
            jnp.swapaxes(dv, 1, 2).reshape(own, group),
        ],
        axis=0,
    )
    back = dot(joined, jnp.concatenate([wq, wk, wv], axis=1), (((0,), (1,)), ((), ())))
    back = back.astype(jnp.bfloat16)
    if split:
        back = lax.psum_scatter(back, "gx", scatter_dimension=0, tiled=True)
    else:
        back = lax.dynamic_slice_in_dim(back, x_index * (group // gx), group // gx, 0)
    back = lax.psum_scatter(back, "gy", scatter_dimension=0, tiled=True).astype(jnp.float32)
    early_gradient = dot(normed_one, joined, (((0,), (1,)), ((), ()))).astype(jnp.bfloat16)
    early_gradient = jnp.stack(
        [early_gradient[:, :own], early_gradient[:, own : 2 * own], early_gradient[:, 2 * own :]]
    )
    early_gradient = lax.psum(weight_from_heads(early_gradient), "dp").astype(jnp.float32)

    unit_one, inverse_one, _ = normalize(inputs, first_gain_all)
    input_part, first_gain_part = normalize_back(back, unit_one, inverse_one, first_gain_all)
    input_gradient = (middle_gradient + input_part).astype(jnp.bfloat16)

    small = lax.psum(
        (
            first_gain_part,
            second_gain_part,
            jnp.sum(upstream, axis=0),
            jnp.sum(before_gradient, axis=0),
            scale_part,
        ),
        ("dp", "gx", "gy"),
    )
    gain_width, bias_width = first_gain.shape[0], inner_bias.shape[0]
    at_y = lambda a: lax.dynamic_slice_in_dim(a, y_index * gain_width, gain_width, 0)
    return (
        layer_output,
        input_gradient,
        at_y(small[0]),
        small[4] * (softplus_unit / math.sqrt(DH)) * jax.nn.sigmoid(query_scale),
        early_gradient[0],
        early_gradient[1],
        early_gradient[2],
        late_gradient[0].T,
        at_y(small[1]),
        late_gradient[1],
        lax.dynamic_slice_in_dim(small[3], x_index * bias_width, bias_width, 0),
        late_gradient[2].T,
        at_y(small[2]),
    )


def solution(mesh):
    placed = (
        P(("dp", "gx", "gy"), None),
        P("gy"),
        P(),
        P("gy", "gx"),
        P("gy", "gx"),
        P("gy", "gx"),
        P("gx", "gy"),
        P("gy"),
        P("gy", "gx"),
        P("gx"),
        P("gx", "gy"),
        P("gy"),
        P(),
        P(("dp", "gx", "gy"), None),
    )
    return jax.shard_map(
        per_device,
        mesh=mesh,
        in_specs=placed,
        out_specs=(
            P(("dp", "gx", "gy"), None),
            P(("dp", "gx", "gy"), None),
            P("gy"),
            P(),
            P("gy", "gx"),
            P("gy", "gx"),
            P("gy", "gx"),
            P("gx", "gy"),
            P("gy"),
            P("gy", "gx"),
            P("gx"),
            P("gx", "gy"),
            P("gy"),
        ),
        check_vma=False,
    )
```

```python
import functools
import math

import jax
import jax.numpy as jnp
from jax import lax
from jax.experimental import pallas as pl
from jax.experimental.pallas import tpu as pltpu
from jax.sharding import PartitionSpec as P

DH = 80
softplus_unit = 1.442695041
NN = (((1,), (0,)), ((), ()))
NT = (((1,), (1,)), ((), ()))
TN = (((0,), (0,)), ((), ()))


def dot(left, right, how):
    return lax.dot_general(left, right, how, preferred_element_type=jnp.float32)


def visible(scores, i, j, bq, bk, prefix):
    key = j * bk + lax.broadcasted_iota(jnp.int32, scores.shape, 0)
    query = i * bq + lax.broadcasted_iota(jnp.int32, scores.shape, 1)
    return jnp.where((key <= query) | (key < prefix), scores, -1e30)


def block_range(i, bq, bk, prefix):
    whole = jnp.maximum((i * bq + 1) // bk, prefix // bk)
    seen = jnp.maximum(((i + 1) * bq + bk - 1) // bk, (prefix + bk - 1) // bk)
    return whole, seen


def forward_kernel(bq, bk, heads, prefix_ref, q_t, k, v_t, o_t, lse):
    i = pl.program_id(0)
    prefix = prefix_ref[0]
    whole, seen = block_range(i, bq, bk, prefix)

    def step(masked, j, carry):
        out = []
        rows = pl.ds(pl.multiple_of(j * bk, bk), bk)
        scores = [dot(k[h, rows, :], q_t[h], NN) for h in range(heads)]
        for h in range(heads):
            largest, total, mixed = carry[h]
            s = visible(scores[h], i, j, bq, bk, prefix) if masked else scores[h]
            now = jnp.maximum(largest, jnp.max(s, axis=0, keepdims=True))
            raised = jnp.exp(s - now)
            shrink = jnp.exp(largest - now)
            total = total * shrink + jnp.sum(raised, axis=0, keepdims=True)
            mixed = mixed * shrink + dot(v_t[h, :, rows], raised.astype(jnp.bfloat16), NN)
            out.append((now, total, mixed))
        return tuple(out)

    start = tuple(
        (
            jnp.full((1, bq), -1e30, jnp.float32),
            jnp.zeros((1, bq), jnp.float32),
            jnp.zeros((DH, bq), jnp.float32),
        )
        for _ in range(heads)
    )
    done = lax.fori_loop(0, whole, functools.partial(step, False), start)
    done = lax.fori_loop(whole, seen, functools.partial(step, True), done)
    for h in range(heads):
        largest, total, mixed = done[h]
        o_t[h] = mixed / total
        lse[h] = largest + jnp.log(total)


def attention_forward(q_t, k, v_t, prefix):
    heads, _, length = q_t.shape
    bq = bk = min(512, length)
    columns = lambda n: pl.BlockSpec((heads, n, bq), lambda i, p: (0, 0, i))
    whole = lambda a: pl.BlockSpec(a.shape, lambda i, p: (0, 0, 0))
    return pl.pallas_call(
        functools.partial(forward_kernel, bq, bk, heads),
        grid_spec=pltpu.PrefetchScalarGridSpec(
            num_scalar_prefetch=1,
            grid=(length // bq,),
            in_specs=[columns(DH), whole(k), whole(v_t)],
            out_specs=[columns(DH), columns(1)],
        ),
        out_shape=[
            jax.ShapeDtypeStruct((heads, DH, length), jnp.float32),
            jax.ShapeDtypeStruct((heads, 1, length), jnp.float32),
        ],
        cost_estimate=pl.CostEstimate(
            flops=heads * length * length * 256 * 2,
            transcendentals=heads * length * length // 2,
            bytes_accessed=heads * length * DH * 12,
        ),
        name="attention_forward",
    )(prefix, q_t, k, v_t)


def backward_kernel(
    bq, bk, heads, count, prefix_ref, q_t, k, k_t, v, g_t, o_t, lse, dq_t, dk, dv, dk_sum, dv_sum
):
    i = pl.program_id(0)
    prefix = prefix_ref[0]
    whole, seen = block_range(i, bq, bk, prefix)

    @pl.when(i == 0)
    def _():
        dk_sum[...] = jnp.zeros_like(dk_sum)
        dv_sum[...] = jnp.zeros_like(dv_sum)

    centre = [
        jnp.sum(g_t[h].astype(jnp.float32) * o_t[h], axis=0, keepdims=True) for h in range(heads)
    ]

    def step(masked, j, carry):
        rows = pl.ds(pl.multiple_of(j * bk, bk), bk)
        out = []
        scores = [dot(k[h, rows, :], q_t[h], NN) for h in range(heads)]
        along = [dot(v[h, rows, :], g_t[h], NN) for h in range(heads)]
        for h in range(heads):
            s = visible(scores[h], i, j, bq, bk, prefix) if masked else scores[h]
            weights = jnp.exp(s - lse[h])
            low = (weights * (along[h] - centre[h])).astype(jnp.bfloat16)
            dv_sum[h, rows, :] += dot(weights.astype(jnp.bfloat16), g_t[h], NT)
            dk_sum[h, rows, :] += dot(low, q_t[h], NT)
            out.append(carry[h] + dot(k_t[h, :, rows], low, NN))
        return tuple(out)

    done = tuple(jnp.zeros((DH, bq), jnp.float32) for _ in range(heads))
    done = lax.fori_loop(0, whole, functools.partial(step, False), done)
    done = lax.fori_loop(whole, seen, functools.partial(step, True), done)
    for h in range(heads):
        dq_t[h] = done[h]

    @pl.when(i == count - 1)
    def _():
        dk[...] = dk_sum[...].astype(jnp.bfloat16)
        dv[...] = dv_sum[...].astype(jnp.bfloat16)


def attention_backward(q_t, k, k_t, v, g_t, o_t, lse, prefix):
    heads, _, length = q_t.shape
    bq = bk = min(512, length)
    columns = lambda n: pl.BlockSpec((heads, n, bq), lambda i, p: (0, 0, i))
    whole = lambda a: pl.BlockSpec(a.shape, lambda i, p: (0, 0, 0))
    return pl.pallas_call(
        functools.partial(backward_kernel, bq, bk, heads, length // bq),
        grid_spec=pltpu.PrefetchScalarGridSpec(
            num_scalar_prefetch=1,
            grid=(length // bq,),
            in_specs=[
                columns(DH), whole(k), whole(k_t), whole(v), columns(DH), columns(DH), columns(1)
            ],
            out_specs=[columns(DH), whole(k), whole(k)],
            scratch_shapes=[pltpu.VMEM(k.shape, jnp.float32)] * 2,
        ),
        out_shape=[
            jax.ShapeDtypeStruct(q_t.shape, jnp.float32),
            jax.ShapeDtypeStruct(k.shape, jnp.bfloat16),
            jax.ShapeDtypeStruct(k.shape, jnp.bfloat16),
        ],
        cost_estimate=pl.CostEstimate(
            flops=heads * length * length * 256 * 5,
            transcendentals=heads * length * length // 2,
            bytes_accessed=heads * length * DH * 24,
        ),
        name="attention_backward",
    )(prefix, q_t, k, k_t, v, g_t, o_t, lse)


def late_gradient_kernel(left_a, right_a, left_b, right_b, left_c, right_c, out):
    for n, (left, right) in enumerate(((left_a, right_a), (left_b, right_b), (left_c, right_c))):

        @pl.when(pl.program_id(0) == n)
        def _():
            out[0, :, 0] = (
                dot(left[...], right[...], TN).reshape(out.shape[1:2] + out.shape[3:]).astype(out.dtype)
            )


def late_gradients(pairs, gx, gy):
    rows, wide = pairs[0][0].shape
    tall, own = wide // gy, wide // gx
    left = pl.BlockSpec((rows, wide), lambda w, x: (0, 0))
    right = pl.BlockSpec((rows, own), lambda w, x: (0, x))
    return pl.pallas_call(
        late_gradient_kernel,
        grid=(3, gx),
        in_specs=[left, right] * 3,
        out_specs=pl.BlockSpec((1, gy, 1, tall, own), lambda w, x: (x, 0, w, 0, 0)),
        out_shape=jax.ShapeDtypeStruct((gx, gy, 3, tall, own), jnp.bfloat16),
        cost_estimate=pl.CostEstimate(
            flops=6 * rows * wide * wide,
            transcendentals=0,
            bytes_accessed=12 * rows * wide + 6 * wide * wide,
        ),
        name="late_gradients",
    )(*[a for pair in pairs for a in pair])

def into(left, blocks):
    return jnp.concatenate([dot(left, b, NN) for b in blocks], axis=1)


def out_of(left, blocks):
    n = blocks.shape[2]
    return sum(dot(left[:, i * n : (i + 1) * n], b, NT) for i, b in enumerate(blocks))


def normalize(values, gain):
    inverse = lax.rsqrt(jnp.mean(values * values, axis=-1, keepdims=True) + 1e-06)
    unit = values * inverse
    return unit, inverse, (unit * gain).astype(jnp.bfloat16)


def normalize_back(upstream, unit, inverse, gain):
    scaled = upstream * gain
    mean = jnp.mean(scaled * unit, axis=-1, keepdims=True)
    return inverse * (scaled - unit * mean), jnp.sum(upstream * unit, axis=0)


def per_device(
    layer_input,
    first_gain,
    query_scale,
    query_weight,
    key_weight,
    value_weight,
    output_weight,
    second_gain,
    inner_weight,
    inner_bias,
    outer_weight,
    outer_bias,
    prefix_len,
    output_cotangent,
):
    gx, gy = lax.axis_size("gx"), lax.axis_size("gy")
    both = ("gx", "gy")
    rows, width = layer_input.shape
    group = rows * gx * gy
    all_heads = query_weight.shape[1] * gx // DH
    split = all_heads % (gx * gy) == 0
    heads = all_heads // (gx * gy if split else gy)
    assert prefix_len.shape[0] == lax.axis_size("dp")
    assert heads * (gx * gy if split else gy) == all_heads
    x_index, y_index = lax.axis_index("gx"), lax.axis_index("gy")
    prefix = lax.dynamic_slice_in_dim(prefix_len, lax.axis_index("dp"), 1, 0)

    def to_heads(columns):
        if split:
            return lax.all_to_all(columns, both, split_axis=0, concat_axis=1, tiled=True)
        half = lax.all_to_all(columns, "gy", split_axis=0, concat_axis=1, tiled=True)
        return lax.all_gather(half, "gx", axis=1, tiled=True)

    def to_tokens(columns):
        if split:
            return lax.all_to_all(columns, both, split_axis=1, concat_axis=0, tiled=True)
        half = lax.dynamic_slice_in_dim(columns, x_index * (group // gx), group // gx, 1)
        return lax.all_to_all(half, "gy", split_axis=1, concat_axis=0, tiled=True)

    def weight_to_heads(stack):
        if not split:
            stack = lax.all_gather(stack, "gx", axis=2, tiled=True)
        return lax.all_to_all(stack, "gy", split_axis=2, concat_axis=1, tiled=True)

    def weight_from_heads(stack):
        stack = lax.all_to_all(stack, "gy", split_axis=1, concat_axis=2, tiled=True)
        if not split:
            own = stack.shape[2] // gx
            stack = lax.dynamic_slice_in_dim(stack, x_index * own, own, 2)
        return stack

    everyone = lax.all_gather(layer_input, both, axis=0, tiled=True)
    own_weights = weight_to_heads(jnp.stack([query_weight, key_weight, value_weight]))
    gains = lax.all_gather(jnp.stack([first_gain, second_gain, outer_bias]), "gy", axis=1, tiled=True)
    inner_bias_all = lax.all_gather(inner_bias, "gx", axis=0, tiled=True)
    first_gain_all, second_gain_all, outer_bias_all = gains[0], gains[1], gains[2]

    late = (output_weight.T, inner_weight, outer_weight.T)
    late, everyone = lax.optimization_barrier((late, everyone))
    output_all, inner_all, outer_all = (
        lax.all_gather(w, both, axis=0, tiled=False).reshape(gx, gy * w.shape[0], w.shape[1])
        for w in late
    )

    _, _, normed_one = normalize(everyone.astype(jnp.float32), first_gain_all)
    factor = jax.nn.softplus(query_scale) * (softplus_unit / math.sqrt(DH))
    own = heads * DH
    wq, wk, wv = own_weights[0], own_weights[1], own_weights[2]
    turned = dot(jnp.concatenate([wq, wk, wv], axis=1), normed_one, (((0,), (1,)), ((), ())))
    queries_t = turned[:own].reshape(heads, DH, group)
    k_t = turned[own : 2 * own].reshape(heads, DH, group).astype(jnp.bfloat16)
    v_t = turned[2 * own :].reshape(heads, DH, group).astype(jnp.bfloat16)
    q_t = (queries_t * factor[None, :, None]).astype(jnp.bfloat16)
    k = jnp.swapaxes(k_t, 1, 2)
    v = jnp.swapaxes(v_t, 1, 2)
    o_t, lse = attention_forward(q_t, k, v_t, prefix)
    attended = to_tokens(o_t.reshape(own, group).astype(jnp.bfloat16))

    inputs = layer_input.astype(jnp.float32)
    attended = attended.T
    middle = inputs + out_of(attended, output_all)
    unit_two, inverse_two, normed_two = normalize(middle, second_gain_all)
    before = into(normed_two, inner_all) + inner_bias_all
    sigmoid = jax.nn.sigmoid(before)
    hidden = (before * sigmoid).astype(jnp.bfloat16)
    layer_output = (middle + out_of(hidden, outer_all) + outer_bias_all).astype(jnp.bfloat16)

    upstream = output_cotangent.astype(jnp.float32)
    hidden_gradient = into(output_cotangent, outer_all)
    before_gradient = hidden_gradient * sigmoid * (1.0 + before * (1.0 - sigmoid))
    before_low = before_gradient.astype(jnp.bfloat16)
    middle_part, second_gain_part = normalize_back(
        out_of(before_low, inner_all), unit_two, inverse_two, second_gain_all
    )
    middle_gradient = upstream + middle_part
    branch_low = middle_gradient.astype(jnp.bfloat16)
    g_t = to_heads(into(branch_low, output_all).astype(jnp.bfloat16).T)

    late_gradient = late_gradients(
        ((branch_low, attended), (normed_two, before_low), (output_cotangent, hidden)), gx, gy
    )
    late_gradient = late_gradient.reshape((gx * gy,) + late_gradient.shape[2:])
    late_gradient = lax.psum_scatter(late_gradient, both, scatter_dimension=0, tiled=False)
    late_gradient = lax.psum(late_gradient, "dp")

    dq_t, dk, dv = attention_backward(
        q_t, k, k_t, v, g_t.reshape(heads, DH, group), o_t, lse, prefix
    )
    scale_part = jnp.sum(dq_t * queries_t, axis=(0, 2))
    if not split:
        scale_part = scale_part / gx
    joined = jnp.concatenate(
        [
            (dq_t * factor[None, :, None]).astype(jnp.bfloat16).reshape(own, group),
            jnp.swapaxes(dk, 1, 2).reshape(own, group),
            jnp.swapaxes(dv, 1, 2).reshape(own, group),
        ],
        axis=0,
    )
    back = dot(joined, jnp.concatenate([wq, wk, wv], axis=1), (((0,), (1,)), ((), ())))
    back = back.astype(jnp.bfloat16)
    if split:
        back = lax.psum_scatter(back, "gx", scatter_dimension=0, tiled=True)
    else:
        back = lax.dynamic_slice_in_dim(back, x_index * (group // gx), group // gx, 0)
    back = lax.psum_scatter(back, "gy", scatter_dimension=0, tiled=True).astype(jnp.float32)
    early_gradient = dot(normed_one, joined, (((0,), (1,)), ((), ()))).astype(jnp.bfloat16)
    early_gradient = jnp.stack(
        [early_gradient[:, :own], early_gradient[:, own : 2 * own], early_gradient[:, 2 * own :]]
    )
    early_gradient = weight_from_heads(early_gradient)
    early_gradient, late_gradient = lax.optimization_barrier((early_gradient, late_gradient))
    early_gradient = lax.psum(early_gradient, "dp").astype(jnp.float32)
    late_gradient = late_gradient.astype(jnp.float32)

    unit_one, inverse_one, _ = normalize(inputs, first_gain_all)
    input_part, first_gain_part = normalize_back(back, unit_one, inverse_one, first_gain_all)
    input_gradient = (middle_gradient + input_part).astype(jnp.bfloat16)

    small = lax.psum(
        (
            first_gain_part,
            second_gain_part,
            jnp.sum(upstream, axis=0),
            jnp.sum(before_gradient, axis=0),
            scale_part,
        ),
        ("dp", "gx", "gy"),
    )
    gain_width, bias_width = first_gain.shape[0], inner_bias.shape[0]
    at_y = lambda a: lax.dynamic_slice_in_dim(a, y_index * gain_width, gain_width, 0)
    return (
        layer_output,
        input_gradient,
        at_y(small[0]),
        small[4] * (softplus_unit / math.sqrt(DH)) * jax.nn.sigmoid(query_scale),
        early_gradient[0],
        early_gradient[1],
        early_gradient[2],
        late_gradient[0].T,
        at_y(small[1]),
        late_gradient[1],
        lax.dynamic_slice_in_dim(small[3], x_index * bias_width, bias_width, 0),
        late_gradient[2].T,
        at_y(small[2]),
    )


def solution(mesh):
    placed = (
        P(("dp", "gx", "gy"), None),
        P("gy"),
        P(),
        P("gy", "gx"),
        P("gy", "gx"),
        P("gy", "gx"),
        P("gx", "gy"),
        P("gy"),
        P("gy", "gx"),
        P("gx"),
        P("gx", "gy"),
        P("gy"),
        P(),
        P(("dp", "gx", "gy"), None),
    )
    return jax.shard_map(
        per_device,
        mesh=mesh,
        in_specs=placed,
        out_specs=(
            P(("dp", "gx", "gy"), None),
            P(("dp", "gx", "gy"), None),
            P("gy"),
            P(),
            P("gy", "gx"),
            P("gy", "gx"),
            P("gy", "gx"),
            P("gx", "gy"),
            P("gy"),
            P("gy", "gx"),
            P("gx"),
            P("gx", "gy"),
            P("gy"),
        ),
        check_vma=False,
    )
```

```python
import functools
import math

import jax
import jax.numpy as jnp
from jax import lax
from jax.experimental import pallas as pl
from jax.experimental.pallas import tpu as pltpu
from jax.sharding import PartitionSpec as P

DH = 80
softplus_unit = 1.442695041
NN = (((1,), (0,)), ((), ()))
NT = (((1,), (1,)), ((), ()))
TN = (((0,), (0,)), ((), ()))


def dot(left, right, how):
    return lax.dot_general(left, right, how, preferred_element_type=jnp.float32)


def visible(scores, i, j, bq, bk, prefix):
    key = j * bk + lax.broadcasted_iota(jnp.int32, scores.shape, 0)
    query = i * bq + lax.broadcasted_iota(jnp.int32, scores.shape, 1)
    return jnp.where((key <= query) | (key < prefix), scores, -1e30)


def block_range(i, bq, bk, prefix):
    whole = jnp.maximum((i * bq + 1) // bk, prefix // bk)
    seen = jnp.maximum(((i + 1) * bq + bk - 1) // bk, (prefix + bk - 1) // bk)
    return whole, seen


def forward_kernel(bq, bk, heads, prefix_ref, q_t, k, v_t, o_t, lse):
    i = pl.program_id(0)
    prefix = prefix_ref[0]
    whole, seen = block_range(i, bq, bk, prefix)

    def step(masked, j, carry):
        out = []
        rows = pl.ds(pl.multiple_of(j * bk, bk), bk)
        scores = [dot(k[h, rows, :], q_t[h], NN) for h in range(heads)]
        for h in range(heads):
            largest, total, mixed = carry[h]
            s = visible(scores[h], i, j, bq, bk, prefix) if masked else scores[h]
            now = jnp.maximum(largest, jnp.max(s, axis=0, keepdims=True))
            raised = jnp.exp(s - now)
            shrink = jnp.exp(largest - now)
            total = total * shrink + jnp.sum(raised, axis=0, keepdims=True)
            mixed = mixed * shrink + dot(v_t[h, :, rows], raised.astype(jnp.bfloat16), NN)
            out.append((now, total, mixed))
        return tuple(out)

    start = tuple(
        (
            jnp.full((1, bq), -1e30, jnp.float32),
            jnp.zeros((1, bq), jnp.float32),
            jnp.zeros((DH, bq), jnp.float32),
        )
        for _ in range(heads)
    )
    done = lax.fori_loop(0, whole, functools.partial(step, False), start)
    done = lax.fori_loop(whole, seen, functools.partial(step, True), done)
    for h in range(heads):
        largest, total, mixed = done[h]
        o_t[h] = mixed / total
        lse[h] = largest + jnp.log(total)


def attention_forward(q_t, k, v_t, prefix):
    heads, _, length = q_t.shape
    bq = bk = min(512, length)
    columns = lambda n: pl.BlockSpec((heads, n, bq), lambda i, p: (0, 0, i))
    whole = lambda a: pl.BlockSpec(a.shape, lambda i, p: (0, 0, 0))
    return pl.pallas_call(
        functools.partial(forward_kernel, bq, bk, heads),
        grid_spec=pltpu.PrefetchScalarGridSpec(
            num_scalar_prefetch=1,
            grid=(length // bq,),
            in_specs=[columns(DH), whole(k), whole(v_t)],
            out_specs=[columns(DH), columns(1)],
        ),
        out_shape=[
            jax.ShapeDtypeStruct((heads, DH, length), jnp.float32),
            jax.ShapeDtypeStruct((heads, 1, length), jnp.float32),
        ],
        cost_estimate=pl.CostEstimate(
            flops=heads * length * length * 256 * 2,
            transcendentals=heads * length * length // 2,
            bytes_accessed=heads * length * DH * 12,
        ),
        name="attention_forward",
    )(prefix, q_t, k, v_t)


def backward_kernel(
    bq, bk, heads, count, prefix_ref, factor, queries_t, q_t, k, k_t, v, g_t, o_t, lse,
    joined, scale, dk_sum, dv_sum, scale_sum,
):
    i = pl.program_id(0)
    prefix = prefix_ref[0]
    whole, seen = block_range(i, bq, bk, prefix)

    @pl.when(i == 0)
    def _():
        dk_sum[...] = jnp.zeros_like(dk_sum)
        dv_sum[...] = jnp.zeros_like(dv_sum)
        scale_sum[...] = jnp.zeros_like(scale_sum)

    centre = [
        jnp.sum(g_t[h].astype(jnp.float32) * o_t[h], axis=0, keepdims=True) for h in range(heads)
    ]

    def step(masked, j, carry):
        rows = pl.ds(pl.multiple_of(j * bk, bk), bk)
        out = []
        for h in range(heads):
            s = dot(k[h, rows, :], q_t[h], NN)
            along = dot(v[h, rows, :], g_t[h], NN)
            s = visible(s, i, j, bq, bk, prefix) if masked else s
            weights = jnp.exp(s - lse[h])
            low = (weights * (along - centre[h])).astype(jnp.bfloat16)
            dv_sum[h, :, rows] += dot(g_t[h], weights.astype(jnp.bfloat16), NT)
            dk_sum[h, :, rows] += dot(q_t[h], low, NT)
            out.append(carry[h] + dot(k_t[h, :, rows], low, NN))
        return tuple(out)

    done = tuple(jnp.zeros((DH, bq), jnp.float32) for _ in range(heads))
    done = lax.fori_loop(0, whole, functools.partial(step, False), done)
    done = lax.fori_loop(whole, seen, functools.partial(step, True), done)
    own = pl.ds(pl.multiple_of(i * bq, bq), bq)
    for h in range(heads):
        joined[h * DH : (h + 1) * DH, own] = (done[h] * factor[...]).astype(jnp.bfloat16)
        scale_sum[...] += done[h] * queries_t[h]

    @pl.when(i == count - 1)
    def _():
        for h in range(heads):
            joined[(heads + h) * DH : (heads + h + 1) * DH, :] = dk_sum[h].astype(jnp.bfloat16)
            joined[(2 * heads + h) * DH : (2 * heads + h + 1) * DH, :] = dv_sum[h].astype(jnp.bfloat16)
        scale[...] = jnp.sum(scale_sum[...], axis=1, keepdims=True)


def attention_backward(factor, queries_t, q_t, k, k_t, v, g_t, o_t, lse, prefix):
    heads, _, length = q_t.shape
    bq = bk = min(512, length)
    columns = lambda n: pl.BlockSpec((heads, n, bq), lambda i, p: (0, 0, i))
    whole = lambda a: pl.BlockSpec(a.shape, lambda i, p: (0,) * len(a.shape))
    joined = jax.ShapeDtypeStruct((3 * heads * DH, length), jnp.bfloat16)
    scale = jax.ShapeDtypeStruct((DH, 1), jnp.float32)
    return pl.pallas_call(
        functools.partial(backward_kernel, bq, bk, heads, length // bq),
        grid_spec=pltpu.PrefetchScalarGridSpec(
            num_scalar_prefetch=1,
            grid=(length // bq,),
            in_specs=[
                whole(factor), columns(DH), columns(DH), whole(k), whole(k_t), whole(v),
                columns(DH), columns(DH), columns(1),
            ],
            out_specs=[whole(joined), whole(scale)],
            scratch_shapes=[pltpu.VMEM(k_t.shape, jnp.float32)] * 2 + [pltpu.VMEM((DH, bq), jnp.float32)],
        ),
        out_shape=[joined, scale],
        cost_estimate=pl.CostEstimate(
            flops=heads * length * length * 256 * 5,
            transcendentals=heads * length * length // 2,
            bytes_accessed=heads * length * DH * 24,
        ),
        name="attention_backward",
    )(prefix, factor, queries_t, q_t, k, k_t, v, g_t, o_t, lse)


MESH = pl.DeviceIdType.MESH


def wide(ref):
    return ref[...].astype(jnp.float32)


def peers():
    x, y, z = lax.axis_index("gx"), lax.axis_index("gy"), lax.axis_index("dp")
    return x, y, z, y + 1 - 2 * (y % 2), (y + 2) % 4, 3 - y, z + 1 - 2 * (z % 2)


def send(src, dst, send_sem, recv_sem, to):
    return pltpu.make_async_remote_copy(
        src_ref=src, dst_ref=dst, send_sem=send_sem, recv_sem=recv_sem, device_id=to, device_id_type=MESH
    )


def greet(devices):
    barrier = pltpu.get_barrier_semaphore()
    for to in devices:
        pl.semaphore_signal(barrier, inc=1, device_id=to, device_id_type=MESH)
    return barrier


def tail_kernel(
    part, dw, back, total,
    mine, theirs, both, first_x, own_x, last_y, first_y, own_y, last_x, mid_x, mid_y,
    pieces, outer, cross, partial, final,
    load, pair_send, pair_recv, give_send, give_recv, xy_send, xy_recv, up_send, up_recv, mid_send, mid_recv, down_send, down_recv,
):
    x, y, z, xn, yn, dn, zn = peers()
    tokens = back.shape[1]
    half = back.shape[0] // 2
    inner = (z == 1) | (z == 2)
    barrier = greet([{"gx": 1 - x}, {"gy": xn}, {"gy": yn}, {"gy": dn}, {"dp": zn}])

    @pl.when(inner)
    def _():
        pl.semaphore_signal(barrier, inc=1, device_id={"dp": 3 - z}, device_id_type=MESH)
        pl.semaphore_wait(barrier, 6)

    @pl.when(jnp.logical_not(inner))
    def _():
        pl.semaphore_wait(barrier, 5)

    def columns(core, owner):
        return part.at[:, pl.ds(pl.multiple_of((core * 4 + owner) * tokens, tokens), tokens)]

    order = (dn, xn, yn, y)
    pair = [send(columns(1 - x, d), theirs.at[n], pair_send.at[n], pair_recv.at[n], {"gx": 1 - x}) for n, d in enumerate(order)]
    loads = [pltpu.make_async_copy(columns(x, d), mine.at[n], load.at[n]) for n, d in enumerate(order)]
    give = [send(dw.at[d], pieces.at[y], give_send.at[n], give_recv.at[n], {"gy": d}) for n, d in enumerate((xn, yn, dn))]
    keep = pltpu.make_async_copy(dw.at[y], pieces.at[y], load.at[4])
    for n in range(4):
        pair[n].start()
        loads[n].start()
        if n == 0:
            keep.start()
            for copy in give:
                copy.start()

    upper, lower = pl.ds(0, half), pl.ds(half, half)
    to_x, to_y = {"gy": xn}, {"gy": yn}
    xy = [
        send(both.at[0, upper, :], first_x, xy_send.at[0], xy_recv.at[0], to_x),
        send(both.at[0, lower, :], first_y, xy_send.at[1], xy_recv.at[1], to_y),
        send(both.at[1, upper, :], own_x, xy_send.at[2], xy_recv.at[2], to_x),
        send(both.at[2, lower, :], own_y, xy_send.at[3], xy_recv.at[3], to_y),
        send(mid_x, last_y, xy_send.at[4], xy_recv.at[4], to_y),
        send(mid_y, last_x, xy_send.at[5], xy_recv.at[5], to_x),
    ]

    for n in range(4):
        loads[n].wait()
        pair[n].wait_recv()
        both[n] = (wide(mine.at[n]) + wide(theirs.at[n])).astype(jnp.bfloat16)
        if n == 0:
            xy[0].start()
            xy[1].start()
        elif n < 3:
            xy[n + 1].start()

    chunk = (y, xn, yn, dn)
    up = [send(pieces.at[c], outer.at[n], up_send.at[n], up_recv.at[n], {"dp": zn}) for n, c in enumerate(chunk)]
    meet = [send(partial.at[n], cross.at[n], mid_send.at[n], mid_recv.at[n], {"dp": 3 - z}) for n in range(4)]
    down = [send(final.at[c], final.at[c], down_send.at[n], down_recv.at[n], {"dp": zn}) for n, c in enumerate(chunk)]

    keep.wait()
    for n in range(4):
        if n:
            give[n - 1].wait_recv()

        @pl.when(jnp.logical_not(inner))
        def _():
            up[n].start()

    def gather_up(n):
        @pl.when(inner)
        def _():
            up[n].wait_recv()
            partial[n] = (wide(pieces.at[chunk[n]]) + wide(outer.at[n])).astype(jnp.bfloat16)
            meet[n].start()

    def send_down(n):
        @pl.when(inner)
        def _():
            meet[n].wait_recv()
            final[chunk[n]] = (wide(partial.at[n]) + wide(cross.at[n])).astype(jnp.bfloat16)
            down[n].start()

    gather_up(0)
    gather_up(1)
    xy[0].wait_recv()
    mid_x[...] = (wide(both.at[2, upper, :]) + wide(first_x)).astype(jnp.bfloat16)
    xy[4].start()
    xy[1].wait_recv()
    mid_y[...] = (wide(both.at[1, lower, :]) + wide(first_y)).astype(jnp.bfloat16)
    xy[5].start()
    send_down(0)
    gather_up(2)
    send_down(1)
    gather_up(3)
    send_down(2)
    send_down(3)
    xy[2].wait_recv()
    xy[4].wait_recv()
    back[0:half, :] = wide(both.at[3, upper, :]) + wide(own_x) + wide(last_y)
    xy[3].wait_recv()
    xy[5].wait_recv()
    back[half : 2 * half, :] = wide(both.at[3, lower, :]) + wide(own_y) + wide(last_x)

    @pl.when(inner)
    def _():
        for n in range(4):
            meet[n].wait_send()
            down[n].wait_send()

    @pl.when(jnp.logical_not(inner))
    def _():
        for n in range(4):
            up[n].wait_send()
            down[n].wait_recv()

    total[...] = final[...]
    for copy in pair + give + xy:
        copy.wait_send()


def tail(part, dw, tokens):
    features = part.shape[0]
    block = pltpu.VMEM((features, tokens), jnp.bfloat16)
    four = pltpu.VMEM((4, features, tokens), jnp.bfloat16)
    half = pltpu.VMEM((features // 2, tokens), jnp.bfloat16)
    blocks = pltpu.VMEM(dw.shape, jnp.bfloat16)
    sem = pltpu.SemaphoreType.DMA
    return pl.pallas_call(
        tail_kernel,
        in_specs=[pl.BlockSpec(memory_space=pl.ANY)] * 2,
        out_specs=[pl.BlockSpec(memory_space=pltpu.VMEM)] * 2,
        out_shape=[
            jax.ShapeDtypeStruct((features, tokens), jnp.float32),
            jax.ShapeDtypeStruct(dw.shape, jnp.bfloat16),
        ],
        scratch_shapes=[four] * 3 + [half] * 8 + [blocks] * 5
        + [sem((5,)), sem((4,)), sem((4,)), sem((3,)), sem((3,)), sem((6,)), sem((6,))]
        + [sem((4,))] * 6,
        compiler_params=pltpu.CompilerParams(collective_id=1, has_side_effects=True),
        name="tail",
    )(part, dw)


def small_sum_kernel(value, out, held, arrived, send_sem, recv_sem):
    x, y, z, xn, yn, dn, zn = peers()
    steps = [{"gx": 1 - x}, {"gy": xn}, {"gy": yn}, {"dp": zn}, {"dp": (z + 2) % 4}]
    barrier = greet(steps)
    pl.semaphore_wait(barrier, 5)
    held[0] = value[...]
    for n, to in enumerate(steps):
        copy = send(held.at[n], arrived.at[n], send_sem.at[n], recv_sem.at[n], to)
        copy.start()
        copy.wait()
        if n < 4:
            held[n + 1] = held[n] + arrived[n]
        else:
            out[...] = held[n] + arrived[n]


def small_sum(value):
    return pl.pallas_call(
        small_sum_kernel,
        in_specs=[pl.BlockSpec(memory_space=pltpu.VMEM)],
        out_specs=pl.BlockSpec(memory_space=pltpu.VMEM),
        out_shape=jax.ShapeDtypeStruct(value.shape, jnp.float32),
        scratch_shapes=[pltpu.VMEM((5,) + value.shape, jnp.float32)] * 2 + [pltpu.SemaphoreType.DMA((5,))] * 2,
        compiler_params=pltpu.CompilerParams(collective_id=2, has_side_effects=True),
        name="small_sum",
    )(value)


def late_gradient_kernel(left_a, right_a, left_b, right_b, left_c, right_c, out):
    for n, (left, right) in enumerate(((left_a, right_a), (left_b, right_b), (left_c, right_c))):

        @pl.when(pl.program_id(0) == n)
        def _():
            out[0, :, 0] = (
                dot(left[...], right[...], TN).reshape(out.shape[1:2] + out.shape[3:]).astype(out.dtype)
            )


def late_gradients(pairs, gx, gy):
    rows, wide = pairs[0][0].shape
    tall, own = wide // gy, wide // gx
    left = pl.BlockSpec((rows, wide), lambda w, x: (0, 0))
    right = pl.BlockSpec((rows, own), lambda w, x: (0, x))
    return pl.pallas_call(
        late_gradient_kernel,
        grid=(3, gx),
        in_specs=[left, right] * 3,
        out_specs=pl.BlockSpec((1, gy, 1, tall, own), lambda w, x: (x, 0, w, 0, 0)),
        out_shape=jax.ShapeDtypeStruct((gx, gy, 3, tall, own), jnp.bfloat16),
        cost_estimate=pl.CostEstimate(
            flops=6 * rows * wide * wide,
            transcendentals=0,
            bytes_accessed=12 * rows * wide + 6 * wide * wide,
        ),
        name="late_gradients",
    )(*[a for pair in pairs for a in pair])

def into(left, blocks):
    return jnp.concatenate([dot(left, b, NN) for b in blocks], axis=1)


def out_of(left, blocks):
    n = blocks.shape[2]
    return sum(dot(left[:, i * n : (i + 1) * n], b, NT) for i, b in enumerate(blocks))


def normalize(values, gain):
    inverse = lax.rsqrt(jnp.mean(values * values, axis=-1, keepdims=True) + 1e-06)
    unit = values * inverse
    return unit, inverse, (unit * gain).astype(jnp.bfloat16)


def normalize_back(upstream, unit, inverse, gain):
    scaled = upstream * gain
    mean = jnp.mean(scaled * unit, axis=-1, keepdims=True)
    return inverse * (scaled - unit * mean), jnp.sum(upstream * unit, axis=0)


def per_device(
    layer_input,
    first_gain,
    query_scale,
    query_weight,
    key_weight,
    value_weight,
    output_weight,
    second_gain,
    inner_weight,
    inner_bias,
    outer_weight,
    outer_bias,
    prefix_len,
    output_cotangent,
):
    gx, gy = lax.axis_size("gx"), lax.axis_size("gy")
    both = ("gx", "gy")
    rows, width = layer_input.shape
    group = rows * gx * gy
    all_heads = query_weight.shape[1] * gx // DH
    split = all_heads % (gx * gy) == 0
    heads = all_heads // (gx * gy if split else gy)
    assert prefix_len.shape[0] == lax.axis_size("dp")
    assert heads * (gx * gy if split else gy) == all_heads
    kernels = split and (gx, gy, lax.axis_size("dp")) == (2, 4, 4)
    x_index, y_index = lax.axis_index("gx"), lax.axis_index("gy")
    prefix = lax.dynamic_slice_in_dim(prefix_len, lax.axis_index("dp"), 1, 0)

    def to_heads(columns):
        if split:
            return lax.all_to_all(columns, both, split_axis=0, concat_axis=1, tiled=True)
        half = lax.all_to_all(columns, "gy", split_axis=0, concat_axis=1, tiled=True)
        return lax.all_gather(half, "gx", axis=1, tiled=True)

    def to_tokens(columns):
        if split:
            return lax.all_to_all(columns, both, split_axis=1, concat_axis=0, tiled=True)
        half = lax.dynamic_slice_in_dim(columns, x_index * (group // gx), group // gx, 1)
        return lax.all_to_all(half, "gy", split_axis=1, concat_axis=0, tiled=True)

    def weight_to_heads(stack):
        if not split:
            stack = lax.all_gather(stack, "gx", axis=2, tiled=True)
        return lax.all_to_all(stack, "gy", split_axis=2, concat_axis=1, tiled=True)

    def weight_from_heads(stack):
        stack = lax.all_to_all(stack, "gy", split_axis=1, concat_axis=2, tiled=True)
        if not split:
            own = stack.shape[2] // gx
            stack = lax.dynamic_slice_in_dim(stack, x_index * own, own, 2)
        return stack

    everyone = lax.all_gather(layer_input, both, axis=0, tiled=True)
    own_weights = weight_to_heads(jnp.stack([query_weight, key_weight, value_weight]))
    gains = lax.all_gather(jnp.stack([first_gain, second_gain, outer_bias]), "gy", axis=1, tiled=True)
    inner_bias_all = lax.all_gather(inner_bias, "gx", axis=0, tiled=True)
    first_gain_all, second_gain_all, outer_bias_all = gains[0], gains[1], gains[2]

    late = (output_weight.T, inner_weight, outer_weight.T)
    late, everyone = lax.optimization_barrier((late, everyone))
    output_all, inner_all, outer_all = (
        lax.all_gather(w, both, axis=0, tiled=False).reshape(gx, gy * w.shape[0], w.shape[1])
        for w in late
    )

    _, _, normed_one = normalize(everyone.astype(jnp.float32), first_gain_all)
    factor = jax.nn.softplus(query_scale) * (softplus_unit / math.sqrt(DH))
    own = heads * DH
    wq, wk, wv = own_weights[0], own_weights[1], own_weights[2]
    turned = dot(jnp.concatenate([wq, wk, wv], axis=1), normed_one, (((0,), (1,)), ((), ())))
    queries_t = turned[:own].reshape(heads, DH, group)
    k_t = turned[own : 2 * own].reshape(heads, DH, group).astype(jnp.bfloat16)
    v_t = turned[2 * own :].reshape(heads, DH, group).astype(jnp.bfloat16)
    q_t = (queries_t * factor[None, :, None]).astype(jnp.bfloat16)
    k = jnp.swapaxes(k_t, 1, 2)
    v = jnp.swapaxes(v_t, 1, 2)
    o_t, lse = attention_forward(q_t, k, v_t, prefix)
    attended = to_tokens(o_t.reshape(own, group).astype(jnp.bfloat16))

    inputs = layer_input.astype(jnp.float32)
    attended = attended.T
    middle = inputs + out_of(attended, output_all)
    unit_two, inverse_two, normed_two = normalize(middle, second_gain_all)
    before = into(normed_two, inner_all) + inner_bias_all
    sigmoid = jax.nn.sigmoid(before)
    hidden = (before * sigmoid).astype(jnp.bfloat16)
    layer_output = (middle + out_of(hidden, outer_all) + outer_bias_all).astype(jnp.bfloat16)

    upstream = output_cotangent.astype(jnp.float32)
    hidden_gradient = into(output_cotangent, outer_all)
    before_gradient = hidden_gradient * sigmoid * (1.0 + before * (1.0 - sigmoid))
    before_low = before_gradient.astype(jnp.bfloat16)
    middle_part, second_gain_part = normalize_back(
        out_of(before_low, inner_all), unit_two, inverse_two, second_gain_all
    )
    middle_gradient = upstream + middle_part
    branch_low = middle_gradient.astype(jnp.bfloat16)
    g_t = to_heads(into(branch_low, output_all).astype(jnp.bfloat16).T)

    late_gradient = late_gradients(
        ((branch_low, attended), (normed_two, before_low), (output_cotangent, hidden)), gx, gy
    )
    late_gradient = late_gradient.reshape((gx * gy,) + late_gradient.shape[2:])
    late_gradient = lax.psum_scatter(late_gradient, both, scatter_dimension=0, tiled=False)
    late_gradient = lax.psum(late_gradient, "dp")

    joined, scale_part = attention_backward(
        factor[:, None], queries_t, q_t, k, k_t, v, g_t.reshape(heads, DH, group), o_t, lse, prefix
    )
    own_all = jnp.concatenate([wq, wk, wv], axis=1)
    part = dot(own_all, joined, NN).astype(jnp.bfloat16)
    early_gradient = dot(normed_one, joined, (((0,), (1,)), ((), ()))).astype(jnp.bfloat16)
    unit_one, inverse_one, _ = normalize(inputs, first_gain_all)
    if kernels:
        back, early_gradient = tail(part, early_gradient.reshape(gy, -1, 3 * own), rows)
        back = back.T
        early_gradient = jnp.moveaxis(
            early_gradient.astype(jnp.float32).reshape(gy, -1, 3, own), 0, 2
        )
        early_gradient = [early_gradient[:, n].reshape(-1, gy * own) for n in range(3)]
        late_gradient = late_gradient.astype(jnp.float32)
    else:
        back = part.T
        if split:
            back = lax.psum_scatter(back, "gx", scatter_dimension=0, tiled=True)
        else:
            back = lax.dynamic_slice_in_dim(back, x_index * (group // gx), group // gx, 0)
        back = lax.psum_scatter(back, "gy", scatter_dimension=0, tiled=True).astype(jnp.float32)
        early_gradient = weight_from_heads(
            jnp.stack([early_gradient[:, n * own : (n + 1) * own] for n in range(3)])
        )
        early_gradient, late_gradient = lax.optimization_barrier((early_gradient, late_gradient))
        early_gradient = lax.psum(early_gradient, "dp").astype(jnp.float32)
        late_gradient = late_gradient.astype(jnp.float32)
    input_part, first_gain_part = normalize_back(back, unit_one, inverse_one, first_gain_all)
    input_gradient = (middle_gradient + input_part).astype(jnp.bfloat16)

    scale_part = scale_part[:, 0] if split else scale_part[:, 0] / gx
    small = [first_gain_part, second_gain_part, jnp.sum(upstream, axis=0), jnp.sum(before_gradient, axis=0)]
    if kernels:
        small = jnp.stack(small + [jnp.pad(scale_part, (0, width - DH))])
        small = small_sum(jnp.pad(small, ((0, 3), (0, 0))))
        small = [small[0], small[1], small[2], small[3], small[4, :DH]]
    else:
        small = lax.psum(tuple(small) + (scale_part,), ("dp", "gx", "gy"))
    gain_width, bias_width = first_gain.shape[0], inner_bias.shape[0]
    at_y = lambda a: lax.dynamic_slice_in_dim(a, y_index * gain_width, gain_width, 0)
    return (
        layer_output,
        input_gradient,
        at_y(small[0]),
        small[4] * (softplus_unit / math.sqrt(DH)) * jax.nn.sigmoid(query_scale),
        early_gradient[0],
        early_gradient[1],
        early_gradient[2],
        late_gradient[0].T,
        at_y(small[1]),
        late_gradient[1],
        lax.dynamic_slice_in_dim(small[3], x_index * bias_width, bias_width, 0),
        late_gradient[2].T,
        at_y(small[2]),
    )


def solution(mesh):
    placed = (
        P(("dp", "gx", "gy"), None),
        P("gy"),
        P(),
        P("gy", "gx"),
        P("gy", "gx"),
        P("gy", "gx"),
        P("gx", "gy"),
        P("gy"),
        P("gy", "gx"),
        P("gx"),
        P("gx", "gy"),
        P("gy"),
        P(),
        P(("dp", "gx", "gy"), None),
    )
    return jax.shard_map(
        per_device,
        mesh=mesh,
        in_specs=placed,
        out_specs=(
            P(("dp", "gx", "gy"), None),
            P(("dp", "gx", "gy"), None),
            P("gy"),
            P(),
            P("gy", "gx"),
            P("gy", "gx"),
            P("gy", "gx"),
            P("gx", "gy"),
            P("gy"),
            P("gy", "gx"),
            P("gx"),
            P("gx", "gy"),
            P("gy"),
        ),
        check_vma=False,
    )
```

```python
import functools
import math

import jax
import jax.numpy as jnp
from jax import lax
from jax.experimental import pallas as pl
from jax.experimental.pallas import tpu as pltpu
from jax.sharding import PartitionSpec as P

DH = 80
softplus_unit = 1.442695041
NN = (((1,), (0,)), ((), ()))
NT = (((1,), (1,)), ((), ()))
TN = (((0,), (0,)), ((), ()))


def dot(left, right, how):
    return lax.dot_general(left, right, how, preferred_element_type=jnp.float32)


def visible(scores, i, j, bq, bk, prefix):
    key = j * bk + lax.broadcasted_iota(jnp.int32, scores.shape, 0)
    query = i * bq + lax.broadcasted_iota(jnp.int32, scores.shape, 1)
    return jnp.where((key <= query) | (key < prefix), scores, -1e30)


def block_range(i, bq, bk, prefix):
    whole = jnp.maximum((i * bq + 1) // bk, prefix // bk)
    seen = jnp.maximum(((i + 1) * bq + bk - 1) // bk, (prefix + bk - 1) // bk)
    return whole, seen


def forward_kernel(bq, bk, heads, prefix_ref, q_t, k, v_t, o_t, lse):
    i = pl.program_id(0)
    prefix = prefix_ref[0]
    whole, seen = block_range(i, bq, bk, prefix)

    def step(masked, j, carry):
        out = []
        rows = pl.ds(pl.multiple_of(j * bk, bk), bk)
        scores = [dot(k[h, rows, :], q_t[h], NN) for h in range(heads)]
        for h in range(heads):
            largest, total, mixed = carry[h]
            s = visible(scores[h], i, j, bq, bk, prefix) if masked else scores[h]
            now = jnp.maximum(largest, jnp.max(s, axis=0, keepdims=True))
            raised = jnp.exp(s - now)
            shrink = jnp.exp(largest - now)
            total = total * shrink + jnp.sum(raised, axis=0, keepdims=True)
            mixed = mixed * shrink + dot(v_t[h, :, rows], raised.astype(jnp.bfloat16), NN)
            out.append((now, total, mixed))
        return tuple(out)

    start = tuple(
        (
            jnp.full((1, bq), -1e30, jnp.float32),
            jnp.zeros((1, bq), jnp.float32),
            jnp.zeros((DH, bq), jnp.float32),
        )
        for _ in range(heads)
    )
    done = lax.fori_loop(0, whole, functools.partial(step, False), start)
    done = lax.fori_loop(whole, seen, functools.partial(step, True), done)
    for h in range(heads):
        largest, total, mixed = done[h]
        o_t[h] = mixed / total
        lse[h] = largest + jnp.log(total)


def attention_forward(q_t, k, v_t, prefix):
    heads, _, length = q_t.shape
    bq = bk = min(512, length)
    columns = lambda n: pl.BlockSpec((heads, n, bq), lambda i, p: (0, 0, i))
    whole = lambda a: pl.BlockSpec(a.shape, lambda i, p: (0, 0, 0))
    return pl.pallas_call(
        functools.partial(forward_kernel, bq, bk, heads),
        grid_spec=pltpu.PrefetchScalarGridSpec(
            num_scalar_prefetch=1,
            grid=(length // bq,),
            in_specs=[columns(DH), whole(k), whole(v_t)],
            out_specs=[columns(DH), columns(1)],
        ),
        out_shape=[
            jax.ShapeDtypeStruct((heads, DH, length), jnp.float32),
            jax.ShapeDtypeStruct((heads, 1, length), jnp.float32),
        ],
        cost_estimate=pl.CostEstimate(
            flops=heads * length * length * 256 * 2,
            transcendentals=heads * length * length // 2,
            bytes_accessed=heads * length * DH * 12,
        ),
        name="attention_forward",
    )(prefix, q_t, k, v_t)


def backward_kernel(
    bq, bk, heads, count, prefix_ref, factor, queries_t, q_t, k, k_t, v, g_t, o_t, lse,
    joined, scale, dk_sum, dv_sum, scale_sum,
):
    i = pl.program_id(0)
    prefix = prefix_ref[0]
    whole, seen = block_range(i, bq, bk, prefix)

    @pl.when(i == 0)
    def _():
        dk_sum[...] = jnp.zeros_like(dk_sum)
        dv_sum[...] = jnp.zeros_like(dv_sum)
        scale_sum[...] = jnp.zeros_like(scale_sum)

    centre = [
        jnp.sum(g_t[h].astype(jnp.float32) * o_t[h], axis=0, keepdims=True) for h in range(heads)
    ]

    def step(masked, j, carry):
        rows = pl.ds(pl.multiple_of(j * bk, bk), bk)
        out = []
        for h in range(heads):
            s = dot(k[h, rows, :], q_t[h], NN)
            along = dot(v[h, rows, :], g_t[h], NN)
            s = visible(s, i, j, bq, bk, prefix) if masked else s
            weights = jnp.exp(s - lse[h])
            low = (weights * (along - centre[h])).astype(jnp.bfloat16)
            dv_sum[h, :, rows] += dot(g_t[h], weights.astype(jnp.bfloat16), NT)
            dk_sum[h, :, rows] += dot(q_t[h], low, NT)
            out.append(carry[h] + dot(k_t[h, :, rows], low, NN))
        return tuple(out)

    done = tuple(jnp.zeros((DH, bq), jnp.float32) for _ in range(heads))
    done = lax.fori_loop(0, whole, functools.partial(step, False), done)
    done = lax.fori_loop(whole, seen, functools.partial(step, True), done)
    own = pl.ds(pl.multiple_of(i * bq, bq), bq)
    for h in range(heads):
        joined[h * DH : (h + 1) * DH, own] = (done[h] * factor[...]).astype(jnp.bfloat16)
        scale_sum[...] += done[h] * queries_t[h]

    @pl.when(i == count - 1)
    def _():
        for h in range(heads):
            joined[(heads + h) * DH : (heads + h + 1) * DH, :] = dk_sum[h].astype(jnp.bfloat16)
            joined[(2 * heads + h) * DH : (2 * heads + h + 1) * DH, :] = dv_sum[h].astype(jnp.bfloat16)
        scale[...] = jnp.sum(scale_sum[...], axis=1, keepdims=True)


def attention_backward(factor, queries_t, q_t, k, k_t, v, g_t, o_t, lse, prefix):
    heads, _, length = q_t.shape
    bq = bk = min(512, length)
    columns = lambda n: pl.BlockSpec((heads, n, bq), lambda i, p: (0, 0, i))
    whole = lambda a: pl.BlockSpec(a.shape, lambda i, p: (0,) * len(a.shape))
    joined = jax.ShapeDtypeStruct((3 * heads * DH, length), jnp.bfloat16)
    scale = jax.ShapeDtypeStruct((DH, 1), jnp.float32)
    return pl.pallas_call(
        functools.partial(backward_kernel, bq, bk, heads, length // bq),
        grid_spec=pltpu.PrefetchScalarGridSpec(
            num_scalar_prefetch=1,
            grid=(length // bq,),
            in_specs=[
                whole(factor), columns(DH), columns(DH), whole(k), whole(k_t), whole(v),
                columns(DH), columns(DH), columns(1),
            ],
            out_specs=[whole(joined), whole(scale)],
            scratch_shapes=[pltpu.VMEM(k_t.shape, jnp.float32)] * 2 + [pltpu.VMEM((DH, bq), jnp.float32)],
        ),
        out_shape=[joined, scale],
        cost_estimate=pl.CostEstimate(
            flops=heads * length * length * 256 * 5,
            transcendentals=heads * length * length // 2,
            bytes_accessed=heads * length * DH * 24,
        ),
        name="attention_backward",
    )(prefix, factor, queries_t, q_t, k, k_t, v, g_t, o_t, lse)


MESH = pl.DeviceIdType.MESH


def wide(ref):
    return ref[...].astype(jnp.float32)


def peers():
    x, y, z = lax.axis_index("gx"), lax.axis_index("gy"), lax.axis_index("dp")
    return x, y, z, y + 1 - 2 * (y % 2), (y + 2) % 4, 3 - y, z + 1 - 2 * (z % 2)


def send(src, dst, send_sem, recv_sem, to):
    return pltpu.make_async_remote_copy(
        src_ref=src, dst_ref=dst, send_sem=send_sem, recv_sem=recv_sem, device_id=to, device_id_type=MESH
    )


def greet(devices):
    barrier = pltpu.get_barrier_semaphore()
    for to in devices:
        pl.semaphore_signal(barrier, inc=1, device_id=to, device_id_type=MESH)
    return barrier


def tail_kernel(
    part, dw, back, total,
    mine, theirs, both, first_x, own_x, last_y, first_y, own_y, last_x, mid_x, mid_y,
    pieces, outer, cross, partial, final,
    load, pair_send, pair_recv, give_send, give_recv, xy_send, xy_recv, up_send, up_recv, mid_send, mid_recv, down_send, down_recv,
):
    x, y, z, xn, yn, dn, zn = peers()
    tokens = back.shape[0]
    half = back.shape[1] // 2
    inner = (z == 1) | (z == 2)
    barrier = greet([{"gx": 1 - x}, {"gy": xn}, {"gy": yn}, {"gy": dn}, {"dp": zn}])

    @pl.when(inner)
    def _():
        pl.semaphore_signal(barrier, inc=1, device_id={"dp": 3 - z}, device_id_type=MESH)
        pl.semaphore_wait(barrier, 6)

    @pl.when(jnp.logical_not(inner))
    def _():
        pl.semaphore_wait(barrier, 5)

    def columns(core, owner):
        return part.at[:, pl.ds(pl.multiple_of((core * 4 + owner) * tokens, tokens), tokens)]

    order = (dn, xn, yn, y)
    pair = [send(columns(1 - x, d), theirs.at[n], pair_send.at[n], pair_recv.at[n], {"gx": 1 - x}) for n, d in enumerate(order)]
    loads = [pltpu.make_async_copy(columns(x, d), mine.at[n], load.at[n]) for n, d in enumerate(order)]
    give = [send(dw.at[d], pieces.at[y], give_send.at[n], give_recv.at[n], {"gy": d}) for n, d in enumerate((xn, yn, dn))]
    keep = pltpu.make_async_copy(dw.at[y], pieces.at[y], load.at[4])
    for n in range(4):
        pair[n].start()
        loads[n].start()
        if n == 0:
            keep.start()
            for copy in give:
                copy.start()

    upper, lower = pl.ds(0, half), pl.ds(half, half)
    to_x, to_y = {"gy": xn}, {"gy": yn}
    xy = [
        send(both.at[0, upper, :], first_x, xy_send.at[0], xy_recv.at[0], to_x),
        send(both.at[0, lower, :], first_y, xy_send.at[1], xy_recv.at[1], to_y),
        send(both.at[1, upper, :], own_x, xy_send.at[2], xy_recv.at[2], to_x),
        send(both.at[2, lower, :], own_y, xy_send.at[3], xy_recv.at[3], to_y),
        send(mid_x, last_y, xy_send.at[4], xy_recv.at[4], to_y),
        send(mid_y, last_x, xy_send.at[5], xy_recv.at[5], to_x),
    ]

    for n in range(4):
        loads[n].wait()
        pair[n].wait_recv()
        both[n] = (wide(mine.at[n]) + wide(theirs.at[n])).astype(jnp.bfloat16)
        if n == 0:
            xy[0].start()
            xy[1].start()
        elif n < 3:
            xy[n + 1].start()

    chunk = (y, xn, yn, dn)
    up = [send(pieces.at[c], outer.at[n], up_send.at[n], up_recv.at[n], {"dp": zn}) for n, c in enumerate(chunk)]
    meet = [send(partial.at[n], cross.at[n], mid_send.at[n], mid_recv.at[n], {"dp": 3 - z}) for n in range(4)]
    down = [send(final.at[c], final.at[c], down_send.at[n], down_recv.at[n], {"dp": zn}) for n, c in enumerate(chunk)]

    keep.wait()
    for n in range(4):
        if n:
            give[n - 1].wait_recv()

        @pl.when(jnp.logical_not(inner))
        def _():
            up[n].start()

    def gather_up(n):
        @pl.when(inner)
        def _():
            up[n].wait_recv()
            partial[n] = (wide(pieces.at[chunk[n]]) + wide(outer.at[n])).astype(jnp.bfloat16)
            meet[n].start()

    def send_down(n):
        @pl.when(inner)
        def _():
            meet[n].wait_recv()
            final[chunk[n]] = (wide(partial.at[n]) + wide(cross.at[n])).astype(jnp.bfloat16)
            down[n].start()

    gather_up(0)
    gather_up(1)
    xy[0].wait_recv()
    mid_x[...] = (wide(both.at[2, upper, :]) + wide(first_x)).astype(jnp.bfloat16)
    xy[4].start()
    xy[1].wait_recv()
    mid_y[...] = (wide(both.at[1, lower, :]) + wide(first_y)).astype(jnp.bfloat16)
    xy[5].start()
    send_down(0)
    gather_up(2)
    send_down(1)
    gather_up(3)
    send_down(2)
    send_down(3)
    xy[2].wait_recv()
    xy[4].wait_recv()
    back[:, 0:half] = (wide(both.at[3, upper, :]) + wide(own_x) + wide(last_y)).T
    xy[3].wait_recv()
    xy[5].wait_recv()
    back[:, half : 2 * half] = (wide(both.at[3, lower, :]) + wide(own_y) + wide(last_x)).T

    @pl.when(inner)
    def _():
        for n in range(4):
            meet[n].wait_send()
            down[n].wait_send()

    @pl.when(jnp.logical_not(inner))
    def _():
        for n in range(4):
            up[n].wait_send()
            down[n].wait_recv()

    total[...] = final[...]
    for copy in pair + give + xy:
        copy.wait_send()


def tail(part, dw, tokens):
    features = part.shape[0]
    block = pltpu.VMEM((features, tokens), jnp.bfloat16)
    four = pltpu.VMEM((4, features, tokens), jnp.bfloat16)
    half = pltpu.VMEM((features // 2, tokens), jnp.bfloat16)
    blocks = pltpu.VMEM(dw.shape, jnp.bfloat16)
    sem = pltpu.SemaphoreType.DMA
    return pl.pallas_call(
        tail_kernel,
        in_specs=[pl.BlockSpec(memory_space=pl.ANY)] * 2,
        out_specs=[pl.BlockSpec(memory_space=pltpu.VMEM)] * 2,
        out_shape=[
            jax.ShapeDtypeStruct((tokens, features), jnp.float32),
            jax.ShapeDtypeStruct(dw.shape, jnp.bfloat16),
        ],
        scratch_shapes=[four] * 3 + [half] * 8 + [blocks] * 5
        + [sem((5,)), sem((4,)), sem((4,)), sem((3,)), sem((3,)), sem((6,)), sem((6,))]
        + [sem((4,))] * 6,
        compiler_params=pltpu.CompilerParams(collective_id=1, has_side_effects=True),
        cost_estimate=pl.CostEstimate(flops=60_000_000_000, transcendentals=0, bytes_accessed=180_000_000),
        name="tail",
    )(part, dw)


def small_sum_kernel(value, out, held, arrived, send_sem, recv_sem):
    x, y, z, xn, yn, dn, zn = peers()
    steps = [{"gx": 1 - x}, {"gy": xn}, {"gy": yn}, {"dp": zn}, {"dp": (z + 2) % 4}]
    barrier = greet(steps)
    pl.semaphore_wait(barrier, 5)
    held[0] = value[...]
    for n, to in enumerate(steps):
        copy = send(held.at[n], arrived.at[n], send_sem.at[n], recv_sem.at[n], to)
        copy.start()
        copy.wait()
        if n < 4:
            held[n + 1] = held[n] + arrived[n]
        else:
            out[...] = held[n] + arrived[n]


def small_sum(value):
    return pl.pallas_call(
        small_sum_kernel,
        in_specs=[pl.BlockSpec(memory_space=pltpu.VMEM)],
        out_specs=pl.BlockSpec(memory_space=pltpu.VMEM),
        out_shape=jax.ShapeDtypeStruct(value.shape, jnp.float32),
        scratch_shapes=[pltpu.VMEM((5,) + value.shape, jnp.float32)] * 2 + [pltpu.SemaphoreType.DMA((5,))] * 2,
        compiler_params=pltpu.CompilerParams(collective_id=2, has_side_effects=True),
        cost_estimate=pl.CostEstimate(flops=12_000_000_000, transcendentals=0, bytes_accessed=36_000_000),
        name="small_sum",
    )(value)


def head_kernel(
    rows_in, blocks_in, small_in, scale_factor,
    normed, weights, small, queries_t, q_t, k_t, v_t, k, v,
    gathered, kept, weights_t, arrived,
    load, keep_send, small_send, small_recv, w_send, w_recv, xy_send, xy_recv, pair_send, pair_recv,
):
    x, y, z, xn, yn, dn, zn = peers()
    rows = rows_in.shape[0]
    half = rows // 2
    tall = blocks_in.shape[1]
    heads = q_t.shape[0]
    own = heads * DH
    features = rows_in.shape[1]
    partner, to_x, to_y = {"gx": 1 - x}, {"gy": xn}, {"gy": yn}
    barrier = greet([partner, to_x, to_y, {"gy": dn}])
    pl.semaphore_wait(barrier, 4)

    def block(core, source):
        return gathered.at[pl.ds(pl.multiple_of((core * 4 + source) * rows, rows), rows), :]

    def piece(core, source, lower):
        return gathered.at[pl.ds(pl.multiple_of((core * 4 + source) * rows + lower * half, half), half), :]

    def weight_rows(source):
        return weights.at[pl.ds(pl.multiple_of(source * tall, tall), tall), :]

    upper_in, lower_in = rows_in.at[pl.ds(0, half), :], rows_in.at[pl.ds(half, half), :]
    smalls = [
        send(small_in, arrived.at[n], small_send.at[n], small_recv.at[n], to)
        for n, to in enumerate((to_x, to_y, {"gy": dn}, partner))
    ]
    ws = [
        send(blocks_in.at[d], weight_rows(y), w_send.at[n], w_recv.at[n], {"gy": d})
        for n, d in enumerate((xn, yn, dn))
    ]
    xy = [
        send(lower_in, piece(x, y, 1), xy_send.at[0], xy_recv.at[0], to_x),
        send(upper_in, piece(x, y, 0), xy_send.at[1], xy_recv.at[1], to_y),
        send(upper_in, piece(x, y, 0), xy_send.at[2], xy_recv.at[2], to_x),
        send(lower_in, piece(x, y, 1), xy_send.at[3], xy_recv.at[3], to_y),
        send(piece(x, yn, 0), piece(x, yn, 0), xy_send.at[4], xy_recv.at[4], to_x),
        send(piece(x, xn, 1), piece(x, xn, 1), xy_send.at[5], xy_recv.at[5], to_y),
    ]
    came = ((xn, 1), (yn, 0), (xn, 0), (yn, 1), (dn, 0), (dn, 1))
    pair = [
        send(piece(x, s, lower), piece(x, s, lower), pair_send.at[n], pair_recv.at[n], partner)
        for n, (s, lower) in enumerate(came)
    ] + [send(rows_in, block(x, y), pair_send.at[6], pair_recv.at[6], partner)]
    own_rows = pltpu.make_async_copy(rows_in, block(x, y), load.at[0])
    own_blocks = pltpu.make_async_copy(blocks_in.at[y], weight_rows(y), load.at[1])

    for copy in smalls + [ws[2], ws[0], ws[1], pair[6], own_rows, own_blocks] + xy[:4]:
        copy.start()
    for copy in smalls + ws:
        copy.wait_recv()
    small[...] = small_in[...]
    small[0:3, :] = small_in[0:3, :] + arrived[0, 0:3, :] + arrived[1, 0:3, :] + arrived[2, 0:3, :]
    small[3:4, :] = small_in[3:4, :] + arrived[3, 3:4, :]
    own_blocks.wait()
    weights_t[...] = weights[...].T

    def stage(number, spot):
        def body(u, carry):
            core, odd = u // 2, u % 2
            source, lower = spot(odd)
            start = pl.multiple_of((core * 4 + source) * rows + lower * half, half)
            here = pl.ds(start, half)
            values = wide(gathered.at[here, :])
            inverse = lax.rsqrt(jnp.mean(values * values, axis=-1, keepdims=True) + 1e-06)
            low = (values * inverse * small[0:1, :]).astype(jnp.bfloat16)
            kept[here, :] = low
            pltpu.make_async_copy(kept.at[here, :], normed.at[here, :], keep_send.at[number * 4 + u]).start()
            turned = dot(weights_t[...], low, NT)
            for h in range(heads):
                at = h * DH
                queries_t[h, :, here] = turned[at : at + DH]
                q_t[h, :, here] = (turned[at : at + DH] * scale_factor[...]).astype(jnp.bfloat16)
                key = turned[own + at : own + at + DH]
                value = turned[2 * own + at : 2 * own + at + DH]
                k_t[h, :, here] = key.astype(jnp.bfloat16)
                v_t[h, :, here] = value.astype(jnp.bfloat16)
                k[h, here, :] = key.T.astype(jnp.bfloat16)
                v[h, here, :] = value.T.astype(jnp.bfloat16)
            return carry

        lax.fori_loop(0, 4, body, 0)

    near = lambda odd: xn * (1 - odd) + yn * odd
    own_rows.wait()
    pair[6].wait_recv()
    stage(0, lambda odd: (y, odd))
    for n in range(6):
        xy[n].wait_recv()
        pair[n].start()
        if n < 2:
            xy[5 - n].start()
        if n % 2:
            pair[n - 1].wait_recv()
            pair[n].wait_recv()
            if n == 1:
                stage(1, lambda odd: (near(odd), 1 - odd))
            elif n == 3:
                stage(2, lambda odd: (near(odd), odd))
            else:
                stage(3, lambda odd: (dn, odd))
    for n in range(16):
        pltpu.make_async_copy(kept.at[pl.ds(0, half), :], normed.at[pl.ds(0, half), :], keep_send.at[n]).wait()
    for copy in smalls + ws + xy + pair:
        copy.wait_send()


def head(rows_in, blocks_in, small_in, scale_factor):
    rows, features = rows_in.shape
    three = blocks_in.shape[2]
    heads = three // (3 * DH)
    group = rows * 8
    sem = pltpu.SemaphoreType.DMA
    vmem, anywhere = pl.BlockSpec(memory_space=pltpu.VMEM), pl.BlockSpec(memory_space=pl.ANY)
    low = lambda *shape: jax.ShapeDtypeStruct(shape, jnp.bfloat16)
    return pl.pallas_call(
        head_kernel,
        in_specs=[anywhere, anywhere, vmem, vmem],
        out_specs=[anywhere] + [vmem] * 8,
        out_shape=[
            low(group, features),
            low(features, three),
            jax.ShapeDtypeStruct(small_in.shape, jnp.float32),
            jax.ShapeDtypeStruct((heads, DH, group), jnp.float32),
            low(heads, DH, group),
            low(heads, DH, group),
            low(heads, DH, group),
            low(heads, group, DH),
            low(heads, group, DH),
        ],
        scratch_shapes=[
            pltpu.VMEM((group, features), jnp.bfloat16),
            pltpu.VMEM((group, features), jnp.bfloat16),
            pltpu.VMEM((three, features), jnp.bfloat16),
            pltpu.VMEM((4,) + small_in.shape, jnp.float32),
        ]
        + [sem((2,)), sem((16,)), sem((4,)), sem((4,)), sem((3,)), sem((3,)), sem((6,)), sem((6,)), sem((7,)), sem((7,))],
        compiler_params=pltpu.CompilerParams(collective_id=3, has_side_effects=True),
        cost_estimate=pl.CostEstimate(flops=60_000_000_000, transcendentals=0, bytes_accessed=180_000_000),
        name="head",
    )(rows_in, blocks_in, small_in, scale_factor)


def late_gradient_kernel(left_a, right_a, left_b, right_b, left_c, right_c, out):
    for n, (left, right) in enumerate(((left_a, right_a), (left_b, right_b), (left_c, right_c))):

        @pl.when(pl.program_id(0) == n)
        def _():
            out[0, :, 0] = (
                dot(left[...], right[...], TN).reshape(out.shape[1:2] + out.shape[3:]).astype(out.dtype)
            )


def late_gradients(pairs, gx, gy):
    rows, wide = pairs[0][0].shape
    tall, own = wide // gy, wide // gx
    left = pl.BlockSpec((rows, wide), lambda w, x: (0, 0))
    right = pl.BlockSpec((rows, own), lambda w, x: (0, x))
    return pl.pallas_call(
        late_gradient_kernel,
        grid=(3, gx),
        in_specs=[left, right] * 3,
        out_specs=pl.BlockSpec((1, gy, 1, tall, own), lambda w, x: (x, 0, w, 0, 0)),
        out_shape=jax.ShapeDtypeStruct((gx, gy, 3, tall, own), jnp.bfloat16),
        cost_estimate=pl.CostEstimate(
            flops=6 * rows * wide * wide,
            transcendentals=0,
            bytes_accessed=12 * rows * wide + 6 * wide * wide,
        ),
        name="late_gradients",
    )(*[a for pair in pairs for a in pair])

def into(left, blocks):
    return jnp.concatenate([dot(left, b, NN) for b in blocks], axis=1)


def out_of(left, blocks):
    n = blocks.shape[2]
    return sum(dot(left[:, i * n : (i + 1) * n], b, NT) for i, b in enumerate(blocks))


def normalize(values, gain):
    inverse = lax.rsqrt(jnp.mean(values * values, axis=-1, keepdims=True) + 1e-06)
    unit = values * inverse
    return unit, inverse, (unit * gain).astype(jnp.bfloat16)


def normalize_back(upstream, unit, inverse, gain):
    scaled = upstream * gain
    mean = jnp.mean(scaled * unit, axis=-1, keepdims=True)
    return inverse * (scaled - unit * mean), jnp.sum(upstream * unit, axis=0)


def per_device(
    layer_input,
    first_gain,
    query_scale,
    query_weight,
    key_weight,
    value_weight,
    output_weight,
    second_gain,
    inner_weight,
    inner_bias,
    outer_weight,
    outer_bias,
    prefix_len,
    output_cotangent,
):
    gx, gy = lax.axis_size("gx"), lax.axis_size("gy")
    both = ("gx", "gy")
    rows, width = layer_input.shape
    group = rows * gx * gy
    all_heads = query_weight.shape[1] * gx // DH
    split = all_heads % (gx * gy) == 0
    heads = all_heads // (gx * gy if split else gy)
    assert prefix_len.shape[0] == lax.axis_size("dp")
    assert heads * (gx * gy if split else gy) == all_heads
    kernels = split and (gx, gy, lax.axis_size("dp")) == (2, 4, 4)
    x_index, y_index = lax.axis_index("gx"), lax.axis_index("gy")
    prefix = lax.dynamic_slice_in_dim(prefix_len, lax.axis_index("dp"), 1, 0)

    def to_heads(columns):
        if split:
            return lax.all_to_all(columns, both, split_axis=0, concat_axis=1, tiled=True)
        half = lax.all_to_all(columns, "gy", split_axis=0, concat_axis=1, tiled=True)
        return lax.all_gather(half, "gx", axis=1, tiled=True)

    def to_tokens(columns):
        if split:
            return lax.all_to_all(columns, both, split_axis=1, concat_axis=0, tiled=True)
        half = lax.dynamic_slice_in_dim(columns, x_index * (group // gx), group // gx, 1)
        return lax.all_to_all(half, "gy", split_axis=1, concat_axis=0, tiled=True)

    def weight_to_heads(stack):
        if not split:
            stack = lax.all_gather(stack, "gx", axis=2, tiled=True)
        return lax.all_to_all(stack, "gy", split_axis=2, concat_axis=1, tiled=True)

    def weight_from_heads(stack):
        stack = lax.all_to_all(stack, "gy", split_axis=1, concat_axis=2, tiled=True)
        if not split:
            own = stack.shape[2] // gx
            stack = lax.dynamic_slice_in_dim(stack, x_index * own, own, 2)
        return stack

    factor = jax.nn.softplus(query_scale) * (softplus_unit / math.sqrt(DH))
    own = heads * DH
    late = (output_weight.T, inner_weight, outer_weight.T)
    if kernels:
        blocks = jnp.stack([query_weight, key_weight, value_weight], axis=1)
        blocks = blocks.reshape(-1, 3, gy, own).transpose(2, 0, 1, 3).reshape(gy, -1, 3 * own)
        small = jnp.stack([first_gain, second_gain, outer_bias])
        small = lax.dynamic_update_slice(
            jnp.zeros((8, width), jnp.float32), small, (0, y_index * first_gain.shape[0])
        )
        small = lax.dynamic_update_slice(
            small, inner_bias[None], (3, x_index * inner_bias.shape[0])
        )
        normed_one, own_all, small, queries_t, q_t, k_t, v_t, k, v = head(
            layer_input, blocks, small, factor[:, None]
        )
        first_gain_all, second_gain_all, outer_bias_all, inner_bias_all = small[0], small[1], small[2], small[3]
        late, q_t = lax.optimization_barrier((late, q_t))
    else:
        everyone = lax.all_gather(layer_input, both, axis=0, tiled=True)
        own_weights = weight_to_heads(jnp.stack([query_weight, key_weight, value_weight]))
        gains = lax.all_gather(jnp.stack([first_gain, second_gain, outer_bias]), "gy", axis=1, tiled=True)
        inner_bias_all = lax.all_gather(inner_bias, "gx", axis=0, tiled=True)
        first_gain_all, second_gain_all, outer_bias_all = gains[0], gains[1], gains[2]
        late, everyone = lax.optimization_barrier((late, everyone))
        _, _, normed_one = normalize(everyone.astype(jnp.float32), first_gain_all)
        own_all = jnp.concatenate([own_weights[0], own_weights[1], own_weights[2]], axis=1)
        turned = dot(own_all, normed_one, (((0,), (1,)), ((), ())))
        queries_t = turned[:own].reshape(heads, DH, group)
        k_t = turned[own : 2 * own].reshape(heads, DH, group).astype(jnp.bfloat16)
        v_t = turned[2 * own :].reshape(heads, DH, group).astype(jnp.bfloat16)
        q_t = (queries_t * factor[None, :, None]).astype(jnp.bfloat16)
        k = jnp.swapaxes(k_t, 1, 2)
        v = jnp.swapaxes(v_t, 1, 2)
    output_all, inner_all, outer_all = (
        lax.all_gather(w, both, axis=0, tiled=False).reshape(gx, gy * w.shape[0], w.shape[1])
        for w in late
    )
    o_t, lse = attention_forward(q_t, k, v_t, prefix)
    attended = to_tokens(o_t.reshape(own, group).astype(jnp.bfloat16))

    inputs = layer_input.astype(jnp.float32)
    attended = attended.T
    middle = inputs + out_of(attended, output_all)
    unit_two, inverse_two, normed_two = normalize(middle, second_gain_all)
    before = into(normed_two, inner_all) + inner_bias_all
    sigmoid = jax.nn.sigmoid(before)
    hidden = (before * sigmoid).astype(jnp.bfloat16)
    layer_output = (middle + out_of(hidden, outer_all) + outer_bias_all).astype(jnp.bfloat16)

    upstream = output_cotangent.astype(jnp.float32)
    hidden_gradient = into(output_cotangent, outer_all)
    before_gradient = hidden_gradient * sigmoid * (1.0 + before * (1.0 - sigmoid))
    before_low = before_gradient.astype(jnp.bfloat16)
    middle_part, second_gain_part = normalize_back(
        out_of(before_low, inner_all), unit_two, inverse_two, second_gain_all
    )
    middle_gradient = upstream + middle_part
    branch_low = middle_gradient.astype(jnp.bfloat16)
    g_t = to_heads(into(branch_low, output_all).astype(jnp.bfloat16).T)

    late_gradient = late_gradients(
        ((branch_low, attended), (normed_two, before_low), (output_cotangent, hidden)), gx, gy
    )
    late_gradient = late_gradient.reshape((gx * gy,) + late_gradient.shape[2:])
    late_gradient = lax.psum_scatter(late_gradient, both, scatter_dimension=0, tiled=False)

    joined, scale_part = attention_backward(
        factor[:, None], queries_t, q_t, k, k_t, v, g_t.reshape(heads, DH, group), o_t, lse, prefix
    )
    late_gradient, joined = lax.optimization_barrier((late_gradient, joined))
    late_gradient = lax.psum(late_gradient, "dp")
    part = dot(own_all, joined, NN).astype(jnp.bfloat16)
    early_gradient = dot(normed_one, joined, (((0,), (1,)), ((), ()))).astype(jnp.bfloat16)
    unit_one, inverse_one, _ = normalize(inputs, first_gain_all)
    if kernels:
        back, early_gradient = tail(part, early_gradient.reshape(gy, -1, 3 * own), rows)
        early_gradient = jnp.moveaxis(
            early_gradient.astype(jnp.float32).reshape(gy, -1, 3, own), 0, 2
        )
        early_gradient = [early_gradient[:, n].reshape(-1, gy * own) for n in range(3)]
        late_gradient = late_gradient.astype(jnp.float32)
    else:
        back = part.T
        if split:
            back = lax.psum_scatter(back, "gx", scatter_dimension=0, tiled=True)
        else:
            back = lax.dynamic_slice_in_dim(back, x_index * (group // gx), group // gx, 0)
        back = lax.psum_scatter(back, "gy", scatter_dimension=0, tiled=True).astype(jnp.float32)
        early_gradient = weight_from_heads(
            jnp.stack([early_gradient[:, n * own : (n + 1) * own] for n in range(3)])
        )
        early_gradient, late_gradient = lax.optimization_barrier((early_gradient, late_gradient))
        early_gradient = lax.psum(early_gradient, "dp").astype(jnp.float32)
        late_gradient = late_gradient.astype(jnp.float32)
    input_part, first_gain_part = normalize_back(back, unit_one, inverse_one, first_gain_all)
    input_gradient = (middle_gradient + input_part).astype(jnp.bfloat16)

    scale_part = scale_part[:, 0] if split else scale_part[:, 0] / gx
    small = [first_gain_part, second_gain_part, jnp.sum(upstream, axis=0), jnp.sum(before_gradient, axis=0)]
    if kernels:
        small = jnp.stack(small + [jnp.pad(scale_part, (0, width - DH))])
        small = small_sum(jnp.pad(small, ((0, 3), (0, 0))))
        small = [small[0], small[1], small[2], small[3], small[4, :DH]]
    else:
        small = lax.psum(tuple(small) + (scale_part,), ("dp", "gx", "gy"))
    gain_width, bias_width = first_gain.shape[0], inner_bias.shape[0]
    at_y = lambda a: lax.dynamic_slice_in_dim(a, y_index * gain_width, gain_width, 0)
    return (
        layer_output,
        input_gradient,
        at_y(small[0]),
        small[4] * (softplus_unit / math.sqrt(DH)) * jax.nn.sigmoid(query_scale),
        early_gradient[0],
        early_gradient[1],
        early_gradient[2],
        late_gradient[0].T,
        at_y(small[1]),
        late_gradient[1],
        lax.dynamic_slice_in_dim(small[3], x_index * bias_width, bias_width, 0),
        late_gradient[2].T,
        at_y(small[2]),
    )


def solution(mesh):
    placed = (
        P(("dp", "gx", "gy"), None),
        P("gy"),
        P(),
        P("gy", "gx"),
        P("gy", "gx"),
        P("gy", "gx"),
        P("gx", "gy"),
        P("gy"),
        P("gy", "gx"),
        P("gx"),
        P("gx", "gy"),
        P("gy"),
        P(),
        P(("dp", "gx", "gy"), None),
    )
    return jax.shard_map(
        per_device,
        mesh=mesh,
        in_specs=placed,
        out_specs=(
            P(("dp", "gx", "gy"), None),
            P(("dp", "gx", "gy"), None),
            P("gy"),
            P(),
            P("gy", "gx"),
            P("gy", "gx"),
            P("gy", "gx"),
            P("gx", "gy"),
            P("gy"),
            P("gy", "gx"),
            P("gx"),
            P("gx", "gy"),
            P("gy"),
        ),
        check_vma=False,
    )
```

```python
import functools
import math

import jax
import jax.numpy as jnp
from jax import lax
from jax.experimental import pallas as pl
from jax.experimental.pallas import tpu as pltpu
from jax.sharding import PartitionSpec as P

DH = 80
softplus_unit = 1.442695041
NN = (((1,), (0,)), ((), ()))
NT = (((1,), (1,)), ((), ()))
TN = (((0,), (0,)), ((), ()))


def dot(left, right, how):
    return lax.dot_general(left, right, how, preferred_element_type=jnp.float32)


def visible(scores, i, j, bq, bk, prefix):
    key = j * bk + lax.broadcasted_iota(jnp.int32, scores.shape, 0)
    query = i * bq + lax.broadcasted_iota(jnp.int32, scores.shape, 1)
    return jnp.where((key <= query) | (key < prefix), scores, -1e30)


def block_range(i, bq, bk, prefix):
    whole = jnp.maximum((i * bq + 1) // bk, prefix // bk)
    seen = jnp.maximum(((i + 1) * bq + bk - 1) // bk, (prefix + bk - 1) // bk)
    return whole, seen


def forward_kernel(bq, bk, heads, prefix_ref, q_t, k, v_t, o_t, lse):
    i = pl.program_id(0)
    prefix = prefix_ref[0]
    whole, seen = block_range(i, bq, bk, prefix)

    def step(masked, j, carry):
        out = []
        rows = pl.ds(pl.multiple_of(j * bk, bk), bk)
        scores = [dot(k[h, rows, :], q_t[h], NN) for h in range(heads)]
        for h in range(heads):
            largest, total, mixed = carry[h]
            s = visible(scores[h], i, j, bq, bk, prefix) if masked else scores[h]
            now = jnp.maximum(largest, jnp.max(s, axis=0, keepdims=True))
            raised = jnp.exp(s - now)
            shrink = jnp.exp(largest - now)
            total = total * shrink + jnp.sum(raised, axis=0, keepdims=True)
            mixed = mixed * shrink + dot(v_t[h, :, rows], raised.astype(jnp.bfloat16), NN)
            out.append((now, total, mixed))
        return tuple(out)

    start = tuple(
        (
            jnp.full((1, bq), -1e30, jnp.float32),
            jnp.zeros((1, bq), jnp.float32),
            jnp.zeros((DH, bq), jnp.float32),
        )
        for _ in range(heads)
    )
    done = lax.fori_loop(0, whole, functools.partial(step, False), start)
    done = lax.fori_loop(whole, seen, functools.partial(step, True), done)
    for h in range(heads):
        largest, total, mixed = done[h]
        o_t[h] = mixed / total
        lse[h] = largest + jnp.log(total)


def attention_forward(q_t, k, v_t, prefix):
    heads, _, length = q_t.shape
    bq = bk = min(512, length)
    columns = lambda n: pl.BlockSpec((heads, n, bq), lambda i, p: (0, 0, i))
    whole = lambda a: pl.BlockSpec(a.shape, lambda i, p: (0, 0, 0))
    return pl.pallas_call(
        functools.partial(forward_kernel, bq, bk, heads),
        grid_spec=pltpu.PrefetchScalarGridSpec(
            num_scalar_prefetch=1,
            grid=(length // bq,),
            in_specs=[columns(DH), whole(k), whole(v_t)],
            out_specs=[columns(DH), columns(1)],
        ),
        out_shape=[
            jax.ShapeDtypeStruct((heads, DH, length), jnp.float32),
            jax.ShapeDtypeStruct((heads, 1, length), jnp.float32),
        ],
        cost_estimate=pl.CostEstimate(
            flops=heads * length * length * 256 * 2,
            transcendentals=heads * length * length // 2,
            bytes_accessed=heads * length * DH * 12,
        ),
        name="attention_forward",
    )(prefix, q_t, k, v_t)


def backward_kernel(
    bq, bk, heads, count, prefix_ref, factor, queries_t, q_t, k, k_t, v, g_t, o_t, lse,
    joined, scale, dk_sum, dv_sum, scale_sum,
):
    i = pl.program_id(0)
    prefix = prefix_ref[0]
    whole, seen = block_range(i, bq, bk, prefix)

    @pl.when(i == 0)
    def _():
        dk_sum[...] = jnp.zeros_like(dk_sum)
        dv_sum[...] = jnp.zeros_like(dv_sum)
        scale_sum[...] = jnp.zeros_like(scale_sum)

    centre = [
        jnp.sum(g_t[h].astype(jnp.float32) * o_t[h], axis=0, keepdims=True) for h in range(heads)
    ]

    def step(masked, j, carry):
        rows = pl.ds(pl.multiple_of(j * bk, bk), bk)
        out = []
        for h in range(heads):
            s = dot(k[h, rows, :], q_t[h], NN)
            along = dot(v[h, rows, :], g_t[h], NN)
            s = visible(s, i, j, bq, bk, prefix) if masked else s
            weights = jnp.exp(s - lse[h])
            low = (weights * (along - centre[h])).astype(jnp.bfloat16)
            dv_sum[h, :, rows] += dot(g_t[h], weights.astype(jnp.bfloat16), NT)
            dk_sum[h, :, rows] += dot(q_t[h], low, NT)
            out.append(carry[h] + dot(k_t[h, :, rows], low, NN))
        return tuple(out)

    done = tuple(jnp.zeros((DH, bq), jnp.float32) for _ in range(heads))
    done = lax.fori_loop(0, whole, functools.partial(step, False), done)
    done = lax.fori_loop(whole, seen, functools.partial(step, True), done)
    own = pl.ds(pl.multiple_of(i * bq, bq), bq)
    for h in range(heads):
        joined[h * DH : (h + 1) * DH, own] = (done[h] * factor[...]).astype(jnp.bfloat16)
        scale_sum[...] += done[h] * queries_t[h]

    @pl.when(i == count - 1)
    def _():
        for h in range(heads):
            joined[(heads + h) * DH : (heads + h + 1) * DH, :] = dk_sum[h].astype(jnp.bfloat16)
            joined[(2 * heads + h) * DH : (2 * heads + h + 1) * DH, :] = dv_sum[h].astype(jnp.bfloat16)
        scale[...] = jnp.sum(scale_sum[...], axis=1, keepdims=True)


def attention_backward(factor, queries_t, q_t, k, k_t, v, g_t, o_t, lse, prefix):
    heads, _, length = q_t.shape
    bq = bk = min(512, length)
    columns = lambda n: pl.BlockSpec((heads, n, bq), lambda i, p: (0, 0, i))
    whole = lambda a: pl.BlockSpec(a.shape, lambda i, p: (0,) * len(a.shape))
    joined = jax.ShapeDtypeStruct((3 * heads * DH, length), jnp.bfloat16)
    scale = jax.ShapeDtypeStruct((DH, 1), jnp.float32)
    return pl.pallas_call(
        functools.partial(backward_kernel, bq, bk, heads, length // bq),
        grid_spec=pltpu.PrefetchScalarGridSpec(
            num_scalar_prefetch=1,
            grid=(length // bq,),
            in_specs=[
                whole(factor), columns(DH), columns(DH), whole(k), whole(k_t), whole(v),
                columns(DH), columns(DH), columns(1),
            ],
            out_specs=[whole(joined), whole(scale)],
            scratch_shapes=[pltpu.VMEM(k_t.shape, jnp.float32)] * 2 + [pltpu.VMEM((DH, bq), jnp.float32)],
        ),
        out_shape=[joined, scale],
        cost_estimate=pl.CostEstimate(
            flops=heads * length * length * 256 * 5,
            transcendentals=heads * length * length // 2,
            bytes_accessed=heads * length * DH * 24,
        ),
        name="attention_backward",
    )(prefix, factor, queries_t, q_t, k, k_t, v, g_t, o_t, lse)


MESH = pl.DeviceIdType.MESH


def wide(ref):
    return ref[...].astype(jnp.float32)


def peers():
    x, y, z = lax.axis_index("gx"), lax.axis_index("gy"), lax.axis_index("dp")
    return x, y, z, y + 1 - 2 * (y % 2), (y + 2) % 4, 3 - y, z + 1 - 2 * (z % 2)


def send(src, dst, send_sem, recv_sem, to):
    return pltpu.make_async_remote_copy(
        src_ref=src, dst_ref=dst, send_sem=send_sem, recv_sem=recv_sem, device_id=to, device_id_type=MESH
    )


def greet(devices):
    barrier = pltpu.get_barrier_semaphore()
    for to in devices:
        pl.semaphore_signal(barrier, inc=1, device_id=to, device_id_type=MESH)
    return barrier


def tail_kernel(
    part, dw, late, back, total, late_total,
    mine, theirs, both, first_x, own_x, last_y, first_y, own_y, last_x, mid_x, mid_y,
    pieces, outer, cross, partial, final, late_outer, late_cross, late_partial, late_final,
    load, pair_send, pair_recv, give_send, give_recv, xy_send, xy_recv, up_send, up_recv, mid_send, mid_recv, down_send, down_recv,
):
    x, y, z, xn, yn, dn, zn = peers()
    tokens = back.shape[0]
    half = back.shape[1] // 2
    inner = (z == 1) | (z == 2)
    barrier = greet([{"gx": 1 - x}, {"gy": xn}, {"gy": yn}, {"gy": dn}, {"dp": zn}])

    @pl.when(inner)
    def _():
        pl.semaphore_signal(barrier, inc=1, device_id={"dp": 3 - z}, device_id_type=MESH)
        pl.semaphore_wait(barrier, 6)

    @pl.when(jnp.logical_not(inner))
    def _():
        pl.semaphore_wait(barrier, 5)

    late_up = [send(late.at[n], late_outer.at[n], up_send.at[4 + n], up_recv.at[4 + n], {"dp": zn}) for n in range(3)]

    @pl.when(jnp.logical_not(inner))
    def _():
        for copy in late_up:
            copy.start()

    def columns(core, owner):
        return part.at[:, pl.ds(pl.multiple_of((core * 4 + owner) * tokens, tokens), tokens)]

    order = (dn, xn, yn, y)
    pair = [send(columns(1 - x, d), theirs.at[n], pair_send.at[n], pair_recv.at[n], {"gx": 1 - x}) for n, d in enumerate(order)]
    loads = [pltpu.make_async_copy(columns(x, d), mine.at[n], load.at[n]) for n, d in enumerate(order)]
    give = [send(dw.at[d], pieces.at[y], give_send.at[n], give_recv.at[n], {"gy": d}) for n, d in enumerate((xn, yn, dn))]
    keep = pltpu.make_async_copy(dw.at[y], pieces.at[y], load.at[4])
    for n in range(4):
        pair[n].start()
        loads[n].start()
        if n == 0:
            keep.start()
            for copy in give:
                copy.start()

    upper, lower = pl.ds(0, half), pl.ds(half, half)
    to_x, to_y = {"gy": xn}, {"gy": yn}
    xy = [
        send(both.at[0, upper, :], first_x, xy_send.at[0], xy_recv.at[0], to_x),
        send(both.at[0, lower, :], first_y, xy_send.at[1], xy_recv.at[1], to_y),
        send(both.at[1, upper, :], own_x, xy_send.at[2], xy_recv.at[2], to_x),
        send(both.at[2, lower, :], own_y, xy_send.at[3], xy_recv.at[3], to_y),
        send(mid_x, last_y, xy_send.at[4], xy_recv.at[4], to_y),
        send(mid_y, last_x, xy_send.at[5], xy_recv.at[5], to_x),
    ]

    for n in range(4):
        loads[n].wait()
        pair[n].wait_recv()
        both[n] = (wide(mine.at[n]) + wide(theirs.at[n])).astype(jnp.bfloat16)
        if n == 0:
            xy[0].start()
            xy[1].start()
        elif n < 3:
            xy[n + 1].start()

    chunk = (y, xn, yn, dn)
    up = [send(pieces.at[c], outer.at[n], up_send.at[n], up_recv.at[n], {"dp": zn}) for n, c in enumerate(chunk)]
    meet = [send(partial.at[n], cross.at[n], mid_send.at[n], mid_recv.at[n], {"dp": 3 - z}) for n in range(4)]
    down = [send(final.at[c], final.at[c], down_send.at[n], down_recv.at[n], {"dp": zn}) for n, c in enumerate(chunk)]
    late_meet = [send(late_partial.at[n], late_cross.at[n], mid_send.at[4 + n], mid_recv.at[4 + n], {"dp": 3 - z}) for n in range(3)]
    late_down = [send(late_final.at[n], late_final.at[n], down_send.at[4 + n], down_recv.at[4 + n], {"dp": zn}) for n in range(3)]

    keep.wait()
    for n in range(4):
        if n:
            give[n - 1].wait_recv()

        @pl.when(jnp.logical_not(inner))
        def _():
            up[n].start()

    def gather_up(n):
        @pl.when(inner)
        def _():
            up[n].wait_recv()
            partial[n] = (wide(pieces.at[chunk[n]]) + wide(outer.at[n])).astype(jnp.bfloat16)
            meet[n].start()

    def send_down(n):
        @pl.when(inner)
        def _():
            meet[n].wait_recv()
            final[chunk[n]] = (wide(partial.at[n]) + wide(cross.at[n])).astype(jnp.bfloat16)
            down[n].start()

    def late_gather_up(n):
        @pl.when(inner)
        def _():
            late_up[n].wait_recv()
            late_partial[n] = (wide(late.at[n]) + wide(late_outer.at[n])).astype(jnp.bfloat16)
            late_meet[n].start()

    def late_send_down(n):
        @pl.when(inner)
        def _():
            late_meet[n].wait_recv()
            late_final[n] = (wide(late_partial.at[n]) + wide(late_cross.at[n])).astype(jnp.bfloat16)
            late_down[n].start()

    late_gather_up(0)
    late_gather_up(1)
    late_send_down(0)
    xy[0].wait_recv()
    mid_x[...] = (wide(both.at[2, upper, :]) + wide(first_x)).astype(jnp.bfloat16)
    xy[4].start()
    xy[1].wait_recv()
    mid_y[...] = (wide(both.at[1, lower, :]) + wide(first_y)).astype(jnp.bfloat16)
    xy[5].start()
    late_gather_up(2)
    late_send_down(1)
    gather_up(0)
    late_send_down(2)
    gather_up(1)
    send_down(0)
    gather_up(2)
    send_down(1)
    xy[2].wait_recv()
    xy[4].wait_recv()
    back[:, 0:half] = (wide(both.at[3, upper, :]) + wide(own_x) + wide(last_y)).T
    gather_up(3)
    send_down(2)
    xy[3].wait_recv()
    xy[5].wait_recv()
    back[:, half : 2 * half] = (wide(both.at[3, lower, :]) + wide(own_y) + wide(last_x)).T
    send_down(3)

    @pl.when(inner)
    def _():
        for copy in meet + down + late_meet + late_down:
            copy.wait_send()

    @pl.when(jnp.logical_not(inner))
    def _():
        for copy in up + late_up:
            copy.wait_send()
        for copy in down + late_down:
            copy.wait_recv()

    total[...] = final[...]
    late_total[...] = late_final[...]
    for copy in pair + give + xy:
        copy.wait_send()


def tail(part, dw, late, tokens):
    features = part.shape[0]
    block = pltpu.VMEM((4, features, tokens), jnp.bfloat16)
    half = pltpu.VMEM((features // 2, tokens), jnp.bfloat16)
    blocks = pltpu.VMEM(dw.shape, jnp.bfloat16)
    lates = pltpu.VMEM(late.shape, jnp.bfloat16)
    sem = pltpu.SemaphoreType.DMA
    vmem, anywhere = pl.BlockSpec(memory_space=pltpu.VMEM), pl.BlockSpec(memory_space=pl.ANY)
    return pl.pallas_call(
        tail_kernel,
        in_specs=[anywhere, anywhere, vmem],
        out_specs=[vmem] * 3,
        out_shape=[
            jax.ShapeDtypeStruct((tokens, features), jnp.float32),
            jax.ShapeDtypeStruct(dw.shape, jnp.bfloat16),
            jax.ShapeDtypeStruct(late.shape, jnp.bfloat16),
        ],
        scratch_shapes=[block] * 3 + [half] * 8 + [blocks] * 5 + [lates] * 4
        + [sem((5,)), sem((4,)), sem((4,)), sem((3,)), sem((3,)), sem((6,)), sem((6,))]
        + [sem((7,))] * 6,
        compiler_params=pltpu.CompilerParams(collective_id=1, has_side_effects=True),
        cost_estimate=pl.CostEstimate(flops=60_000_000_000, transcendentals=0, bytes_accessed=180_000_000),
        name="tail",
    )(part, dw, late)


def exchange_kernel(
    branch, output_all, attended, normed, before, cotangent, hidden, g_t, late,
    turned, local, send_sem, recv_sem,
):
    x, y, z, xn, yn, dn, zn = peers()
    tokens = branch.shape[0]
    own = g_t.shape[0]
    wide_half = output_all.shape[2]
    spots = (dn, xn, yn, y)
    barrier = greet([{"gx": x if r == 0 else 1 - x, "gy": d} for r in range(2) for d in spots if not (r == 0 and d is y)])
    pl.semaphore_wait(barrier, 7)
    here = pl.ds(pl.multiple_of((x * 4 + y) * tokens, tokens), tokens)
    copies = []
    for r in range(2):
        core = x if r == 0 else 1 - x
        turned[r] = dot(branch[...], output_all[core], NN).T.astype(jnp.bfloat16)
        for n, d in enumerate(spots):
            src = turned.at[r, pl.ds(pl.multiple_of(d * own, own), own), :]
            dst = g_t.at[:, here]
            if r == 0 and n == 3:
                keep = pltpu.make_async_copy(src, dst, local)
                keep.start()
            else:
                at = r * 4 + n - (r == 1)
                copies.append(send(src, dst, send_sem.at[at], recv_sem.at[at], {"gx": core, "gy": d}))
                copies[-1].start()

    def body(c, carry):
        right_at = pl.ds(pl.multiple_of(c * wide_half, wide_half), wide_half)
        for w, (left, right) in enumerate(((branch, attended), (normed, before), (cotangent, hidden))):
            product = dot(left[...], right[:, right_at], TN)
            late[c, :, w] = product.reshape(late.shape[1:2] + late.shape[3:]).astype(jnp.bfloat16)
        return carry

    lax.fori_loop(0, 2, body, 0)
    keep.wait()
    for copy in copies:
        copy.wait()


def exchange(branch, output_all, attended, normed, before, cotangent, hidden, own, gy):
    tokens, features = branch.shape
    gx, _, half = output_all.shape
    vmem = pl.BlockSpec(memory_space=pltpu.VMEM)
    sem = pltpu.SemaphoreType.DMA
    return pl.pallas_call(
        exchange_kernel,
        in_specs=[vmem] * 7,
        out_specs=[vmem] * 2,
        out_shape=[
            jax.ShapeDtypeStruct((own, gx * gy * tokens), jnp.bfloat16),
            jax.ShapeDtypeStruct((gx, gy, 3, features // gy, half), jnp.bfloat16),
        ],
        scratch_shapes=[pltpu.VMEM((gx, half, tokens), jnp.bfloat16), sem, sem((7,)), sem((7,))],
        compiler_params=pltpu.CompilerParams(collective_id=4, has_side_effects=True),
        cost_estimate=pl.CostEstimate(flops=24_000_000_000, transcendentals=0, bytes_accessed=72_000_000),
        name="exchange",
    )(branch, output_all, attended, normed, before, cotangent, hidden)


def small_sum_kernel(value, out, held, arrived, send_sem, recv_sem):
    x, y, z, xn, yn, dn, zn = peers()
    steps = [{"gx": 1 - x}, {"gy": xn}, {"gy": yn}, {"dp": zn}, {"dp": (z + 2) % 4}]
    barrier = greet(steps)
    pl.semaphore_wait(barrier, 5)
    held[0] = value[...]
    for n, to in enumerate(steps):
        copy = send(held.at[n], arrived.at[n], send_sem.at[n], recv_sem.at[n], to)
        copy.start()
        copy.wait()
        if n < 4:
            held[n + 1] = held[n] + arrived[n]
        else:
            out[...] = held[n] + arrived[n]


def small_sum(value):
    return pl.pallas_call(
        small_sum_kernel,
        in_specs=[pl.BlockSpec(memory_space=pltpu.VMEM)],
        out_specs=pl.BlockSpec(memory_space=pltpu.VMEM),
        out_shape=jax.ShapeDtypeStruct(value.shape, jnp.float32),
        scratch_shapes=[pltpu.VMEM((5,) + value.shape, jnp.float32)] * 2 + [pltpu.SemaphoreType.DMA((5,))] * 2,
        compiler_params=pltpu.CompilerParams(collective_id=2, has_side_effects=True),
        cost_estimate=pl.CostEstimate(flops=12_000_000_000, transcendentals=0, bytes_accessed=36_000_000),
        name="small_sum",
    )(value)


def head_kernel(
    rows_in, blocks_in, small_in, scale_factor,
    normed, weights, small, queries_t, q_t, k_t, v_t, k, v,
    gathered, kept, weights_t, arrived,
    load, keep_send, small_send, small_recv, w_send, w_recv, xy_send, xy_recv, pair_send, pair_recv,
):
    x, y, z, xn, yn, dn, zn = peers()
    rows = rows_in.shape[0]
    half = rows // 2
    tall = blocks_in.shape[1]
    heads = q_t.shape[0]
    own = heads * DH
    features = rows_in.shape[1]
    partner, to_x, to_y = {"gx": 1 - x}, {"gy": xn}, {"gy": yn}
    barrier = greet([partner, to_x, to_y, {"gy": dn}])
    pl.semaphore_wait(barrier, 4)

    def block(core, source):
        return gathered.at[pl.ds(pl.multiple_of((core * 4 + source) * rows, rows), rows), :]

    def piece(core, source, lower):
        return gathered.at[pl.ds(pl.multiple_of((core * 4 + source) * rows + lower * half, half), half), :]

    def weight_rows(source):
        return weights.at[pl.ds(pl.multiple_of(source * tall, tall), tall), :]

    upper_in, lower_in = rows_in.at[pl.ds(0, half), :], rows_in.at[pl.ds(half, half), :]
    smalls = [
        send(small_in, arrived.at[n], small_send.at[n], small_recv.at[n], to)
        for n, to in enumerate((to_x, to_y, {"gy": dn}, partner))
    ]
    ws = [
        send(blocks_in.at[d], weight_rows(y), w_send.at[n], w_recv.at[n], {"gy": d})
        for n, d in enumerate((xn, yn, dn))
    ]
    xy = [
        send(lower_in, piece(x, y, 1), xy_send.at[0], xy_recv.at[0], to_x),
        send(upper_in, piece(x, y, 0), xy_send.at[1], xy_recv.at[1], to_y),
        send(upper_in, piece(x, y, 0), xy_send.at[2], xy_recv.at[2], to_x),
        send(lower_in, piece(x, y, 1), xy_send.at[3], xy_recv.at[3], to_y),
        send(piece(x, yn, 0), piece(x, yn, 0), xy_send.at[4], xy_recv.at[4], to_x),
        send(piece(x, xn, 1), piece(x, xn, 1), xy_send.at[5], xy_recv.at[5], to_y),
    ]
    came = ((xn, 1), (yn, 0), (xn, 0), (yn, 1), (dn, 0), (dn, 1))
    pair = [
        send(piece(x, s, lower), piece(x, s, lower), pair_send.at[n], pair_recv.at[n], partner)
        for n, (s, lower) in enumerate(came)
    ] + [send(rows_in, block(x, y), pair_send.at[6], pair_recv.at[6], partner)]
    own_rows = pltpu.make_async_copy(rows_in, block(x, y), load.at[0])
    own_blocks = pltpu.make_async_copy(blocks_in.at[y], weight_rows(y), load.at[1])

    for copy in smalls + [ws[2], ws[0], ws[1], pair[6], own_rows, own_blocks] + xy[:4]:
        copy.start()
    for copy in smalls + ws:
        copy.wait_recv()
    small[...] = small_in[...]
    small[0:3, :] = small_in[0:3, :] + arrived[0, 0:3, :] + arrived[1, 0:3, :] + arrived[2, 0:3, :]
    small[3:4, :] = small_in[3:4, :] + arrived[3, 3:4, :]
    own_blocks.wait()
    weights_t[...] = weights[...].T

    def stage(number, spot):
        def body(u, carry):
            core, odd = u // 2, u % 2
            source, lower = spot(odd)
            start = pl.multiple_of((core * 4 + source) * rows + lower * half, half)
            here = pl.ds(start, half)
            values = wide(gathered.at[here, :])
            inverse = lax.rsqrt(jnp.mean(values * values, axis=-1, keepdims=True) + 1e-06)
            low = (values * inverse * small[0:1, :]).astype(jnp.bfloat16)
            kept[here, :] = low
            pltpu.make_async_copy(kept.at[here, :], normed.at[here, :], keep_send.at[number * 4 + u]).start()
            turned = dot(weights_t[...], low, NT)
            for h in range(heads):
                at = h * DH
                queries_t[h, :, here] = turned[at : at + DH]
                q_t[h, :, here] = (turned[at : at + DH] * scale_factor[...]).astype(jnp.bfloat16)
                key = turned[own + at : own + at + DH]
                value = turned[2 * own + at : 2 * own + at + DH]
                k_t[h, :, here] = key.astype(jnp.bfloat16)
                v_t[h, :, here] = value.astype(jnp.bfloat16)
                k[h, here, :] = key.T.astype(jnp.bfloat16)
                v[h, here, :] = value.T.astype(jnp.bfloat16)
            return carry

        lax.fori_loop(0, 4, body, 0)

    near = lambda odd: xn * (1 - odd) + yn * odd
    own_rows.wait()
    pair[6].wait_recv()
    stage(0, lambda odd: (y, odd))
    for n in range(6):
        xy[n].wait_recv()
        pair[n].start()
        if n < 2:
            xy[5 - n].start()
        if n % 2:
            pair[n - 1].wait_recv()
            pair[n].wait_recv()
            if n == 1:
                stage(1, lambda odd: (near(odd), 1 - odd))
            elif n == 3:
                stage(2, lambda odd: (near(odd), odd))
            else:
                stage(3, lambda odd: (dn, odd))
    for n in range(16):
        pltpu.make_async_copy(kept.at[pl.ds(0, half), :], normed.at[pl.ds(0, half), :], keep_send.at[n]).wait()
    for copy in smalls + ws + xy + pair:
        copy.wait_send()


def head(rows_in, blocks_in, small_in, scale_factor):
    rows, features = rows_in.shape
    three = blocks_in.shape[2]
    heads = three // (3 * DH)
    group = rows * 8
    sem = pltpu.SemaphoreType.DMA
    vmem, anywhere = pl.BlockSpec(memory_space=pltpu.VMEM), pl.BlockSpec(memory_space=pl.ANY)
    low = lambda *shape: jax.ShapeDtypeStruct(shape, jnp.bfloat16)
    return pl.pallas_call(
        head_kernel,
        in_specs=[anywhere, anywhere, vmem, vmem],
        out_specs=[anywhere] + [vmem] * 8,
        out_shape=[
            low(group, features),
            low(features, three),
            jax.ShapeDtypeStruct(small_in.shape, jnp.float32),
            jax.ShapeDtypeStruct((heads, DH, group), jnp.float32),
            low(heads, DH, group),
            low(heads, DH, group),
            low(heads, DH, group),
            low(heads, group, DH),
            low(heads, group, DH),
        ],
        scratch_shapes=[
            pltpu.VMEM((group, features), jnp.bfloat16),
            pltpu.VMEM((group, features), jnp.bfloat16),
            pltpu.VMEM((three, features), jnp.bfloat16),
            pltpu.VMEM((4,) + small_in.shape, jnp.float32),
        ]
        + [sem((2,)), sem((16,)), sem((4,)), sem((4,)), sem((3,)), sem((3,)), sem((6,)), sem((6,)), sem((7,)), sem((7,))],
        compiler_params=pltpu.CompilerParams(collective_id=3, has_side_effects=True),
        cost_estimate=pl.CostEstimate(flops=60_000_000_000, transcendentals=0, bytes_accessed=180_000_000),
        name="head",
    )(rows_in, blocks_in, small_in, scale_factor)


def late_gradient_kernel(left_a, right_a, left_b, right_b, left_c, right_c, out):
    for n, (left, right) in enumerate(((left_a, right_a), (left_b, right_b), (left_c, right_c))):

        @pl.when(pl.program_id(0) == n)
        def _():
            out[0, :, 0] = (
                dot(left[...], right[...], TN).reshape(out.shape[1:2] + out.shape[3:]).astype(out.dtype)
            )


def late_gradients(pairs, gx, gy):
    rows, wide = pairs[0][0].shape
    tall, own = wide // gy, wide // gx
    left = pl.BlockSpec((rows, wide), lambda w, x: (0, 0))
    right = pl.BlockSpec((rows, own), lambda w, x: (0, x))
    return pl.pallas_call(
        late_gradient_kernel,
        grid=(3, gx),
        in_specs=[left, right] * 3,
        out_specs=pl.BlockSpec((1, gy, 1, tall, own), lambda w, x: (x, 0, w, 0, 0)),
        out_shape=jax.ShapeDtypeStruct((gx, gy, 3, tall, own), jnp.bfloat16),
        cost_estimate=pl.CostEstimate(
            flops=6 * rows * wide * wide,
            transcendentals=0,
            bytes_accessed=12 * rows * wide + 6 * wide * wide,
        ),
        name="late_gradients",
    )(*[a for pair in pairs for a in pair])

def into(left, blocks):
    return jnp.concatenate([dot(left, b, NN) for b in blocks], axis=1)


def out_of(left, blocks):
    n = blocks.shape[2]
    return sum(dot(left[:, i * n : (i + 1) * n], b, NT) for i, b in enumerate(blocks))


def normalize(values, gain):
    inverse = lax.rsqrt(jnp.mean(values * values, axis=-1, keepdims=True) + 1e-06)
    unit = values * inverse
    return unit, inverse, (unit * gain).astype(jnp.bfloat16)


def normalize_back(upstream, unit, inverse, gain):
    scaled = upstream * gain
    mean = jnp.mean(scaled * unit, axis=-1, keepdims=True)
    return inverse * (scaled - unit * mean), jnp.sum(upstream * unit, axis=0)


def per_device(
    layer_input,
    first_gain,
    query_scale,
    query_weight,
    key_weight,
    value_weight,
    output_weight,
    second_gain,
    inner_weight,
    inner_bias,
    outer_weight,
    outer_bias,
    prefix_len,
    output_cotangent,
):
    gx, gy = lax.axis_size("gx"), lax.axis_size("gy")
    both = ("gx", "gy")
    rows, width = layer_input.shape
    group = rows * gx * gy
    all_heads = query_weight.shape[1] * gx // DH
    split = all_heads % (gx * gy) == 0
    heads = all_heads // (gx * gy if split else gy)
    assert prefix_len.shape[0] == lax.axis_size("dp")
    assert heads * (gx * gy if split else gy) == all_heads
    kernels = split and (gx, gy, lax.axis_size("dp")) == (2, 4, 4)
    x_index, y_index = lax.axis_index("gx"), lax.axis_index("gy")
    prefix = lax.dynamic_slice_in_dim(prefix_len, lax.axis_index("dp"), 1, 0)

    def to_heads(columns):
        if split:
            return lax.all_to_all(columns, both, split_axis=0, concat_axis=1, tiled=True)
        half = lax.all_to_all(columns, "gy", split_axis=0, concat_axis=1, tiled=True)
        return lax.all_gather(half, "gx", axis=1, tiled=True)

    def to_tokens(columns):
        if split:
            return lax.all_to_all(columns, both, split_axis=1, concat_axis=0, tiled=True)
        half = lax.dynamic_slice_in_dim(columns, x_index * (group // gx), group // gx, 1)
        return lax.all_to_all(half, "gy", split_axis=1, concat_axis=0, tiled=True)

    def weight_to_heads(stack):
        if not split:
            stack = lax.all_gather(stack, "gx", axis=2, tiled=True)
        return lax.all_to_all(stack, "gy", split_axis=2, concat_axis=1, tiled=True)

    def weight_from_heads(stack):
        stack = lax.all_to_all(stack, "gy", split_axis=1, concat_axis=2, tiled=True)
        if not split:
            own = stack.shape[2] // gx
            stack = lax.dynamic_slice_in_dim(stack, x_index * own, own, 2)
        return stack

    factor = jax.nn.softplus(query_scale) * (softplus_unit / math.sqrt(DH))
    own = heads * DH
    late = (output_weight.T, inner_weight, outer_weight.T)
    if kernels:
        blocks = jnp.stack([query_weight, key_weight, value_weight], axis=1)
        blocks = blocks.reshape(-1, 3, gy, own).transpose(2, 0, 1, 3).reshape(gy, -1, 3 * own)
        small = jnp.stack([first_gain, second_gain, outer_bias])
        small = lax.dynamic_update_slice(
            jnp.zeros((8, width), jnp.float32), small, (0, y_index * first_gain.shape[0])
        )
        small = lax.dynamic_update_slice(
            small, inner_bias[None], (3, x_index * inner_bias.shape[0])
        )
        normed_one, own_all, small, queries_t, q_t, k_t, v_t, k, v = head(
            layer_input, blocks, small, factor[:, None]
        )
        first_gain_all, second_gain_all, outer_bias_all, inner_bias_all = small[0], small[1], small[2], small[3]
        late, q_t = lax.optimization_barrier((late, q_t))
    else:
        everyone = lax.all_gather(layer_input, both, axis=0, tiled=True)
        own_weights = weight_to_heads(jnp.stack([query_weight, key_weight, value_weight]))
        gains = lax.all_gather(jnp.stack([first_gain, second_gain, outer_bias]), "gy", axis=1, tiled=True)
        inner_bias_all = lax.all_gather(inner_bias, "gx", axis=0, tiled=True)
        first_gain_all, second_gain_all, outer_bias_all = gains[0], gains[1], gains[2]
        late, everyone = lax.optimization_barrier((late, everyone))
        _, _, normed_one = normalize(everyone.astype(jnp.float32), first_gain_all)
        own_all = jnp.concatenate([own_weights[0], own_weights[1], own_weights[2]], axis=1)
        turned = dot(own_all, normed_one, (((0,), (1,)), ((), ())))
        queries_t = turned[:own].reshape(heads, DH, group)
        k_t = turned[own : 2 * own].reshape(heads, DH, group).astype(jnp.bfloat16)
        v_t = turned[2 * own :].reshape(heads, DH, group).astype(jnp.bfloat16)
        q_t = (queries_t * factor[None, :, None]).astype(jnp.bfloat16)
        k = jnp.swapaxes(k_t, 1, 2)
        v = jnp.swapaxes(v_t, 1, 2)
    output_all, inner_all, outer_all = (
        lax.all_gather(w, both, axis=0, tiled=False).reshape(gx, gy * w.shape[0], w.shape[1])
        for w in late
    )
    o_t, lse = attention_forward(q_t, k, v_t, prefix)
    attended = to_tokens(o_t.reshape(own, group).astype(jnp.bfloat16))

    inputs = layer_input.astype(jnp.float32)
    attended = attended.T
    middle = inputs + out_of(attended, output_all)
    unit_two, inverse_two, normed_two = normalize(middle, second_gain_all)
    before = into(normed_two, inner_all) + inner_bias_all
    sigmoid = jax.nn.sigmoid(before)
    hidden = (before * sigmoid).astype(jnp.bfloat16)
    layer_output = (middle + out_of(hidden, outer_all) + outer_bias_all).astype(jnp.bfloat16)

    upstream = output_cotangent.astype(jnp.float32)
    hidden_gradient = into(output_cotangent, outer_all)
    before_gradient = hidden_gradient * sigmoid * (1.0 + before * (1.0 - sigmoid))
    before_low = before_gradient.astype(jnp.bfloat16)
    middle_part, second_gain_part = normalize_back(
        out_of(before_low, inner_all), unit_two, inverse_two, second_gain_all
    )
    middle_gradient = upstream + middle_part
    branch_low = middle_gradient.astype(jnp.bfloat16)
    if kernels:
        g_t, late_gradient = exchange(
            branch_low, output_all, attended, normed_two, before_low, output_cotangent, hidden, own, gy
        )
    else:
        g_t = to_heads(into(branch_low, output_all).astype(jnp.bfloat16).T)
        late_gradient = late_gradients(
            ((branch_low, attended), (normed_two, before_low), (output_cotangent, hidden)), gx, gy
        )
    late_gradient = late_gradient.reshape((gx * gy,) + late_gradient.shape[2:])
    late_gradient = lax.psum_scatter(late_gradient, both, scatter_dimension=0, tiled=False)

    joined, scale_part = attention_backward(
        factor[:, None], queries_t, q_t, k, k_t, v, g_t.reshape(heads, DH, group), o_t, lse, prefix
    )
    part = dot(own_all, joined, NN).astype(jnp.bfloat16)
    early_gradient = dot(normed_one, joined, (((0,), (1,)), ((), ()))).astype(jnp.bfloat16)
    unit_one, inverse_one, _ = normalize(inputs, first_gain_all)
    if kernels:
        back, early_gradient, late_gradient = tail(
            part, early_gradient.reshape(gy, -1, 3 * own), late_gradient, rows
        )
        early_gradient = jnp.moveaxis(
            early_gradient.astype(jnp.float32).reshape(gy, -1, 3, own), 0, 2
        )
        early_gradient = [early_gradient[:, n].reshape(-1, gy * own) for n in range(3)]
        late_gradient = late_gradient.astype(jnp.float32)
    else:
        back = part.T
        if split:
            back = lax.psum_scatter(back, "gx", scatter_dimension=0, tiled=True)
        else:
            back = lax.dynamic_slice_in_dim(back, x_index * (group // gx), group // gx, 0)
        back = lax.psum_scatter(back, "gy", scatter_dimension=0, tiled=True).astype(jnp.float32)
        early_gradient = weight_from_heads(
            jnp.stack([early_gradient[:, n * own : (n + 1) * own] for n in range(3)])
        )
        late_gradient = lax.psum(late_gradient, "dp")
        early_gradient, late_gradient = lax.optimization_barrier((early_gradient, late_gradient))
        early_gradient = lax.psum(early_gradient, "dp").astype(jnp.float32)
        late_gradient = late_gradient.astype(jnp.float32)
    input_part, first_gain_part = normalize_back(back, unit_one, inverse_one, first_gain_all)
    input_gradient = (middle_gradient + input_part).astype(jnp.bfloat16)

    scale_part = scale_part[:, 0] if split else scale_part[:, 0] / gx
    small = [first_gain_part, second_gain_part, jnp.sum(upstream, axis=0), jnp.sum(before_gradient, axis=0)]
    if kernels:
        small = jnp.stack(small + [jnp.pad(scale_part, (0, width - DH))])
        small = small_sum(jnp.pad(small, ((0, 3), (0, 0))))
        small = [small[0], small[1], small[2], small[3], small[4, :DH]]
    else:
        small = lax.psum(tuple(small) + (scale_part,), ("dp", "gx", "gy"))
    gain_width, bias_width = first_gain.shape[0], inner_bias.shape[0]
    at_y = lambda a: lax.dynamic_slice_in_dim(a, y_index * gain_width, gain_width, 0)
    return (
        layer_output,
        input_gradient,
        at_y(small[0]),
        small[4] * (softplus_unit / math.sqrt(DH)) * jax.nn.sigmoid(query_scale),
        early_gradient[0],
        early_gradient[1],
        early_gradient[2],
        late_gradient[0].T,
        at_y(small[1]),
        late_gradient[1],
        lax.dynamic_slice_in_dim(small[3], x_index * bias_width, bias_width, 0),
        late_gradient[2].T,
        at_y(small[2]),
    )


def solution(mesh):
    placed = (
        P(("dp", "gx", "gy"), None),
        P("gy"),
        P(),
        P("gy", "gx"),
        P("gy", "gx"),
        P("gy", "gx"),
        P("gx", "gy"),
        P("gy"),
        P("gy", "gx"),
        P("gx"),
        P("gx", "gy"),
        P("gy"),
        P(),
        P(("dp", "gx", "gy"), None),
    )
    return jax.shard_map(
        per_device,
        mesh=mesh,
        in_specs=placed,
        out_specs=(
            P(("dp", "gx", "gy"), None),
            P(("dp", "gx", "gy"), None),
            P("gy"),
            P(),
            P("gy", "gx"),
            P("gy", "gx"),
            P("gy", "gx"),
            P("gx", "gy"),
            P("gy"),
            P("gy", "gx"),
            P("gx"),
            P("gx", "gy"),
            P("gy"),
        ),
        check_vma=False,
    )
```
